256 devices in a mesh: blk: 16 (over y_lo, z), tgt: 4 (over y_hi, core), sec: 4 (over x).
Axes of the slice: x: 4, y: 4 (y_hi: 2, y_lo: 2; y = y_hi * 2 + y_lo), z: 8, core: 2. Of those that a mesh axis runs over, the one named last changes fastest.
Arguments:
- modal_loads: bfloat16 [4096, 128], P('blk'), may hold values from -6 to 6
- receptance: bfloat16 [2, 4096, 4096], P(None, ('tgt', 'sec'), 'blk'), may hold values from -0.0625 to 0.0625
- shapes: bfloat16 [32768, 8, 128], P(('blk', 'tgt', 'sec')), may hold values from -0.1875 to 0.1875
- coupling: int32 [256, 8], P(('blk', 'tgt', 'sec')), may hold values from 0 to 31, all different within a row
- panel_coords: float32 [3, 32768], P(None, ('blk', 'tgt', 'sec')), may hold values from 0 to 1
- panel_areas: float32 [32768], P(('blk', 'tgt', 'sec')), may hold values from 0.1 to 1
Outputs:
- new_loads: float32 [4096, 128], P(('blk', 'tgt', 'sec'))
- pressure: bfloat16 [32768, 128], P(('blk', 'tgt', 'sec'))
The draws below stay inside these ranges and needn't reach their ends.
Inputs may be any that keep to these rules, and one draw needn't show every extreme that they name: `coupling`: each row names 8 different mode blocks; every mode block is named by some row.
All inputs are finite; a program needn't handle non-finite values.
Results may differ from the reference program's by a relative error of at most 0.009.
Values may be sent and summed in bfloat16 or wider, within the bound.
A program may use at most 64 MiB of HBM per device.

```python
import math
import jax
import jax.numpy as jnp
from jax import lax

M = 4096
L = 64
MB = 128
K = 8
PBLK = 128
P_SIZE = 32768
NBLK = 256
MBLK = 32


def steps_of(rng, dims, cuts, low, top_value):
    def one(dim, parts):
        steps = jax.random.uniform(jax.random.fold_in(jax.random.fold_in(rng, 6), dim), (parts,), jnp.float32, low / len(cuts), top_value / len(cuts))
        return jnp.repeat(jnp.exp(steps), dims[dim] // parts).reshape((-1,) + (1,) * (len(dims) - dim - 1))

    loudness = one(*cuts[0])
    for cut in cuts[1:]:
        loudness = loudness * one(*cut)
    return loudness


def picks_of(key, rows, count, top, lift):
    sequence = jax.random.permutation(jax.random.fold_in(key, 1), count)
    boost = sequence
    for power in range(3):
        boost = boost * boost // count
    boost = boost * lift // count
    chance = jax.random.randint(jax.random.fold_in(key, 2), (rows, count), 0, 4096) + boost
    sure = jax.random.permutation(jax.random.fold_in(key, 3), rows)[jnp.arange(count) % rows]
    chance = jnp.where(jnp.arange(rows)[:, None] == sure[None, :], 1 << 14, chance)
    priority = chance * count + jnp.arange(count)
    return lax.top_k(priority.astype(jnp.int32), top)[1].astype(jnp.int32)


def bell_draw(rng, dims, deviation, reach, shards=(), dtype=jnp.bfloat16):
    level = steps_of(rng, dims, shards, -0.22, 0.18) if shards else 1.0
    entries = jax.random.normal(rng, dims, jnp.float32) * deviation * level
    return jnp.minimum(jnp.maximum(entries, -reach), reach).astype(dtype)


def setup_inputs(seed: int = 0) -> dict:
    key_of = jax.random.split(jax.random.key(seed), 7)
    return {
        "modal_loads": bell_draw(key_of[0], (M, 2 * L), 1.0, 6.0, ((0, 16),)),
        "receptance": bell_draw(key_of[1], (2, M, M), (2 * M) ** -0.5, 0.0625, ((1, 16), (2, 16))),
        "shapes": bell_draw(key_of[2], (P_SIZE, K, MB), (K * MB) ** -0.5, 0.1875, ((0, 256),)),
        "coupling": picks_of(key_of[3], NBLK, MBLK, K, 2048),
        "panel_coords": jnp.clip(1.0 * jax.random.uniform(key_of[4], (3, P_SIZE), jnp.float32) ** steps_of(key_of[4], (3, P_SIZE), ((1, 256),), -0.2, 0.2), 0.0, 1.0),
        "panel_areas": jnp.clip(jnp.exp(math.log(1.0) - 2.3025851 * jax.random.uniform(key_of[5], (P_SIZE,), jnp.float32) ** steps_of(key_of[5], (P_SIZE,), ((0, 256),), -0.2, 0.2)), 0.1, 1.0),
    }


wave_number = 40.0

def rotate_combine(leading, second):
    half_width = leading.shape[1] // 2
    return jnp.concatenate([leading[:, :half_width] - second[:, half_width:], leading[:, half_width:] + second[:, :half_width]], axis=1)

def pressure_block(target_geometry, source_geometry, source_vel, total_panels):
    delta_x = target_geometry[0][:, None] - source_geometry[0][None, :]
    delta_y = target_geometry[1][:, None] - source_geometry[1][None, :]
    delta_z = target_geometry[2][:, None] - source_geometry[2][None, :]
    source_area = source_geometry[3][None, :]
    distance = jnp.sqrt(delta_x * delta_x + delta_y * delta_y + delta_z * delta_z + source_area / total_panels)
    weight = source_area / (distance * math.sqrt(total_panels))
    phase_angle = wave_number * distance
    kernel = jnp.concatenate([(jnp.cos(phase_angle) * weight).astype(jnp.bfloat16), (jnp.sin(phase_angle) * weight).astype(jnp.bfloat16)], axis=0)
    products = lax.dot_general(kernel, source_vel, (((1,), (1,)), ((), ())), preferred_element_type=jnp.float32)
    target_count = target_geometry.shape[1]
    return rotate_combine(products[:target_count], products[target_count:])

def reference(modal_loads, receptance, shapes, coupling, panel_coords, panel_areas):
    case_width = modal_loads.shape[1]
    stacked = jnp.dot(receptance.reshape(2 * M, M), modal_loads, preferred_element_type=jnp.float32)
    amplitudes = rotate_combine(stacked[:M], stacked[M:]).astype(jnp.bfloat16)
    blocks = amplitudes.reshape(M // MB, MB, case_width)
    chosen = blocks[coupling]
    shaped = shapes.reshape(NBLK, PBLK, K, MB)
    velocity = jnp.einsum('bpkm,bkmc->bpc', shaped.astype(jnp.float32), chosen.astype(jnp.float32)).reshape(P_SIZE, case_width).astype(jnp.bfloat16)
    geometry = jnp.concatenate([panel_coords, panel_areas[None, :]], axis=0)
    vel_t = velocity.T
    block_rows = 256
    target_blocks = geometry.reshape(4, P_SIZE // block_rows, block_rows).transpose(1, 0, 2)

    def single_block(target_geometry):
        return pressure_block(target_geometry, geometry, vel_t, float(P_SIZE))
    pressure_f = lax.map(single_block, target_blocks).reshape(P_SIZE, case_width)
    pressure = pressure_f.astype(jnp.bfloat16)
    weighted = (panel_areas[:, None] * pressure.astype(jnp.float32)).astype(jnp.bfloat16)
    contrib = jnp.einsum('bpkm,bpc->bkmc', shaped.astype(jnp.float32), weighted.reshape(NBLK, PBLK, case_width).astype(jnp.float32))
    summed = jax.ops.segment_sum(contrib.reshape(NBLK * K, MB, case_width), coupling.reshape(-1), M // MB)
    new_loads = summed.reshape(M, case_width)
    return (new_loads, pressure)
```

```python
import functools
import math

import jax
import jax.numpy as jnp
from jax import lax
from jax.experimental import pallas as pl
from jax.experimental.pallas import tpu as pltpu
from jax.sharding import PartitionSpec as P

MESH = pl.DeviceIdType.MESH
F32 = jnp.float32
BF16 = jnp.bfloat16

WAVE = 40.0
YL = 2
PB = 128
CW = 128
RW = 16
ROWS = 64

SIN = (4.442879567546083, -7.307816684491776, 3.5977741780871795, -0.7911993921612632)
COS = (1.4142040148090755, -6.977637323456285, 5.715187874756681, -1.7282138922234693)

GEO_S, GEO_T, RS_AMP, AG_Z, AG_XY, AG_C, RS_PC, RS_PZ, RS_LC, RS_LXY, RS_LZ = range(11)


def horner(coefs, u):
    acc = u * coefs[-1] + coefs[-2]
    for value in coefs[-3::-1]:
        acc = acc * u + value
    return acc


def turn_rows(value):
    n = value.shape[1]
    return jnp.transpose(jnp.broadcast_to(value, (n, n)))


def rotated(value):
    half = value.shape[1] // 2
    turned = pltpu.roll(value, half, 1)
    lane = lax.broadcasted_iota(jnp.int32, value.shape, 1)
    return jnp.where(lane < half, -turned, turned)


def kernel(
    dims,
    loads_ref,
    rec_ref,
    shp_ref,
    cpl_ref,
    crd_ref,
    area_ref,
    out_ref,
    prs_ref,
    geo_s,
    geo_t,
    tgt_b,
    area_b,
    kmat,
    acc,
    part,
    part_h,
    amp_in,
    amp,
    vels,
    w_ref,
    p_out,
    pc_in,
    pz_in,
    shp_t,
    inv,
    cbuf,
    lc_out,
    lc_in,
    lx_out,
    lx_in,
    lx_own,
    lz_out,
    lz_in,
    send_sem,
    recv_sem,
    vsend_sem,
    vrecv_sem,
):
    X, YH, Z, KB = dims
    Y = YH * YL
    n_xy, n_zc, n_blk = X * Y, 2 * Z, YL * Z
    mb = Z * RW
    total_panels = float(PB * 2 * X * Y * Z)

    blk, tgt, sec = lax.axis_index("blk"), lax.axis_index("tgt"), lax.axis_index("sec")
    yl, z = lax.div(blk, Z), lax.rem(blk, Z)
    yh, core = lax.div(tgt, 2), lax.rem(tgt, 2)
    x = sec
    y = yh * YL + yl

    def device(x_, y_, z_, c_):
        return (lax.rem(y_, YL) * Z + z_, lax.div(y_, YL) * 2 + c_, x_)

    def shifted(dx=0, dy=0, dz=0, dc=0):
        return (
            lax.rem(x + dx, X),
            lax.rem(y + dy, Y),
            lax.rem(z + dz, Z),
            lax.rem(core + dc, 2),
        )

    def near(d, n):
        return min(d, n - d)

    xy_steps = sorted(range(1, n_xy), key=lambda q: near(q % X, X) + near(q // X, Y))
    z_steps = sorted(range(1, Z), key=lambda q: near(q, Z))
    zc_steps = [dc * Z + dz for dc in range(2) for dz in range(Z) if dc or dz]
    blk_steps = [dl * Z + dz for dl in range(YL) for dz in range(Z) if dl or dz]

    def yl_place(dl, dz):
        y_ = yh * YL + lax.rem(yl + dl, YL)
        return (x, y_, lax.rem(z + dz, Z), core)

    def send(phase, src, dst, place, send_s=None, recv_s=None):
        copy = pltpu.make_async_remote_copy(
            src_ref=src,
            dst_ref=dst,
            send_sem=send_sem.at[phase] if send_s is None else send_s,
            recv_sem=recv_sem.at[phase] if recv_s is None else recv_s,
            device_id=device(*place),
            device_id_type=MESH,
        )
        copy.start()
        return copy

    def wait_bytes(sem, ref):
        pltpu.make_async_copy(ref, ref, sem).wait()

    barrier = pltpu.get_barrier_semaphore()
    places = [shifted(dx=q % X, dy=q // X) for q in xy_steps]
    places += [shifted(dz=q % Z, dc=q // Z) for q in zc_steps]
    places += [yl_place(q // Z, q % Z) for q in blk_steps if q // Z]
    for place in places:
        pl.semaphore_signal(barrier, inc=1, device_id=device(*place), device_id_type=MESH)

    half_scale = 0.5 * WAVE / math.pi
    geo_s[0, 0:3, :] = crd_ref[...] * half_scale
    geo_s[0, 3:4, :] = area_ref[...] * (half_scale * half_scale / total_panels)
    geo_s[0, 4:8, :] = jnp.zeros((4, PB), F32)
    geo_t[0, :, :] = geo_s[0, :, :]
    loads = loads_ref[...]
    loads_rot = rotated(loads.astype(F32)).astype(BF16)
    psum = jnp.dot(rec_ref[0], loads, preferred_element_type=F32) + jnp.dot(
        rec_ref[1], loads_rot, preferred_element_type=F32
    )
    part[...] = psum.reshape(n_blk, RW, CW)
    part_h[...] = psum.astype(BF16).reshape(n_blk, RW, CW)

    pl.semaphore_wait(barrier, len(places))

    for q in reversed(xy_steps):
        send(GEO_S, geo_s.at[0], geo_s.at[q], shifted(dx=q % X, dy=q // X))
    for q in zc_steps:
        send(GEO_T, geo_t.at[0], geo_t.at[q], shifted(dz=q % Z, dc=q // Z))
    for q in blk_steps:
        place = yl_place(q // Z, q % Z)
        owner = lax.rem(place[1], YL) * Z + place[2]
        send(RS_AMP, part_h.at[owner], amp_in.at[q - 1], place)

    area_col = turn_rows(area_ref[...])
    area_b[...] = area_col
    for k in range(KB):
        shp_t[k] = jnp.transpose(shp_ref[k].astype(F32)).astype(BF16)

    def fill_inv(j, carry):
        found = jnp.int32(KB)
        for k in range(KB):
            found = jnp.where(cpl_ref[0, k] == j, jnp.int32(k), found)
        inv[j] = found
        return carry

    lax.fori_loop(0, 2 * YH * X * YL, fill_inv, 0)

    def turn_targets(slot):
        rows = pl.ds(slot * PB, PB)
        for axis in range(3):
            tgt_b[axis, rows, :] = turn_rows(geo_t[slot, axis : axis + 1, :])

    wait_bytes(recv_sem.at[GEO_T], geo_t.at[pl.ds(1, n_zc - 1)])

    def turn_step(slot, carry):
        turn_targets(slot)
        return carry

    lax.fori_loop(0, n_zc, turn_step, 0)
    wait_bytes(recv_sem.at[GEO_S], geo_s.at[pl.ds(1, n_xy - 1)])

    steps = n_zc * PB // ROWS

    def kernel_chunks(lo, hi):
        def chunk(d, carry):
            shape = (ROWS, PB)
            sx = jnp.broadcast_to(geo_s[d, 0:1, :], shape)
            sy = jnp.broadcast_to(geo_s[d, 1:2, :], shape)
            sz = jnp.broadcast_to(geo_s[d, 2:3, :], shape)
            sa = jnp.broadcast_to(geo_s[d, 3:4, :], shape)

            def rows_step(i, inner):
                rows = pl.ds(pl.multiple_of(i * ROWS, ROWS), ROWS)
                dx = tgt_b[0, rows, :] - sx
                dy = tgt_b[1, rows, :] - sy
                dz = tgt_b[2, rows, :] - sz
                d2 = dx * dx + dy * dy + dz * dz + sa
                r = lax.rsqrt(d2)
                h = d2 * r
                f = h - jnp.round(h)
                u = f * f
                s = horner(SIN, u) * f
                c = horner(COS, u)
                rs = r * s
                kmat[d, rows, 0:PB] = (r - rs * s).astype(BF16)
                kmat[d, rows, PB : 2 * PB] = (rs * c).astype(BF16)
                return inner

            return lax.fori_loop(0, steps, rows_step, carry)

        lax.fori_loop(lo, hi, chunk, 0)

    cuts = [round(n_xy * part_of / 16) for part_of in (0, 3, 6, 12, 14, 16)]

    kernel_chunks(cuts[0], cuts[1])

    wait_bytes(recv_sem.at[RS_AMP], amp_in)
    asum = part[blk]
    for q in range(n_blk - 1):
        asum = asum + amp_in[q].astype(F32)
    xl = x * YL + yl
    amp[yh, core, xl, z] = asum.astype(BF16)
    for dz in reversed(z_steps):
        mine = amp.at[yh, core, xl, z]
        send(AG_Z, mine, mine, shifted(dz=dz))

    kernel_chunks(cuts[1], cuts[2])
    wait_bytes(recv_sem.at[AG_Z], amp.at[0, 0, 0, pl.ds(0, Z - 1)])
    for q in reversed(xy_steps):
        mine = amp.at[yh, core, xl]
        send(AG_XY, mine, mine, shifted(dx=q % X, dy=q // X))

    kernel_chunks(cuts[2], cuts[3])
    for _ in range(1):
        wait_bytes(recv_sem.at[AG_XY], kmat.at[0, pl.ds(0, (n_xy - 1) * mb * CW // (2 * PB)), :])
    mine = amp.at[:, core]
    send(AG_C, mine, mine, shifted(dc=1))
    kernel_chunks(cuts[3], cuts[4])
    wait_bytes(recv_sem.at[AG_C], mine)

    vel = jnp.zeros((PB, CW), F32)
    for k in range(KB):
        j = cpl_ref[0, k]
        jl = lax.rem(j, X * YL)
        jc = lax.rem(lax.div(j, X * YL), 2)
        jh = lax.div(j, X * YL * 2)
        block = amp[jh, jc, jl].reshape(mb, CW)
        vel = vel + jnp.dot(shp_ref[k], block, preferred_element_type=F32)
    vels[0] = (vel * area_b[...] * (half_scale / math.sqrt(total_panels))).astype(BF16)
    for q in reversed(xy_steps):
        send(
            0,
            vels.at[0],
            vels.at[q],
            shifted(dx=q % X, dy=q // X),
            vsend_sem.at[0],
            vrecv_sem.at[q - 1],
        )
    kernel_chunks(cuts[4], cuts[5])

    mm_rows = min(512, n_zc * PB)

    def add_chunk(q, first):
        value = vels[q]
        w_ref[0:PB, :] = value
        w_ref[PB : 2 * PB, :] = rotated(value.astype(F32)).astype(BF16)

        def mm_step(i, carry):
            rows = pl.ds(pl.multiple_of(i * mm_rows, mm_rows), mm_rows)
            prod = jnp.dot(kmat[q, rows, :], w_ref[...], preferred_element_type=F32)
            acc[rows, :] = prod if first else acc[rows, :] + prod
            return carry

        lax.fori_loop(0, n_zc * PB // mm_rows, mm_step, 0)

    add_chunk(0, True)
    for q in xy_steps:
        wait_bytes(vrecv_sem.at[q - 1], vels.at[q])
        add_chunk(q, False)

    half = Z * PB
    p_out[...] = acc[half : 2 * half, :].astype(BF16).reshape(Z, PB, CW)
    send(RS_PC, p_out, pc_in, shifted(dc=1))
    wait_bytes(recv_sem.at[RS_PC], pc_in)
    wait_bytes(send_sem.at[RS_PC], p_out)
    for dz in reversed(z_steps):
        rows = slice(dz * PB, (dz + 1) * PB)
        p_out[dz] = (acc[rows, :] + pc_in[dz].astype(F32)).astype(BF16)
        send(RS_PZ, p_out.at[dz], pz_in.at[dz - 1], shifted(dz=Z - dz))
    total = acc[0:PB, :] + pc_in[0].astype(F32)
    wait_bytes(recv_sem.at[RS_PZ], pz_in)
    for dz in range(Z - 1):
        total = total + pz_in[dz].astype(F32)
    pressure = total.astype(BF16)
    prs_ref[...] = pressure
    weighted = (area_b[...] * pressure.astype(F32)).astype(BF16)

    for k in range(KB):
        cbuf[k] = (
            jnp.dot(shp_t[k], weighted, preferred_element_type=F32)
            .astype(BF16)
            .reshape(2, X, RW, CW)
        )
    cbuf[KB] = jnp.zeros((2, X, RW, CW), BF16)
    other = 1 - core
    n_j = YL * Z * YH
    for j in range(n_j):
        lc_out[j] = cbuf[inv[j], other]
    send(RS_LC, lc_out, lc_in, shifted(dc=1))
    wait_bytes(recv_sem.at[RS_LC], lc_in)
    wait_bytes(send_sem.at[RS_LC], lc_out)
    for j in range(n_j):
        jl, jz, jh = j // (Z * YH), j // YH % Z, j % YH
        both = cbuf[inv[j], core].astype(F32) + lc_in[j].astype(F32)
        for xx in range(X):
            lx_own[jl, jh, xx, jz] = both[xx]
            lx_out[jl, jh, xx, jz] = both[xx].astype(BF16)
    for q in reversed(xy_steps):
        place = shifted(dx=q % X, dy=q // X)
        src = lx_out.at[lax.rem(place[1], YL), lax.div(place[1], YL), place[0]]
        send(RS_LXY, src, lx_in.at[q - 1], place)
    wait_bytes(recv_sem.at[RS_LXY], lx_in)
    lsum = lx_own[yl, yh, x]
    for q in range(n_xy - 1):
        lsum = lsum + lx_in[q].astype(F32)
    lx_own[yl, yh, x] = lsum
    lz_out[...] = lsum.astype(BF16)
    for dz in reversed(z_steps):
        place = shifted(dz=dz)
        send(RS_LZ, lz_out.at[place[2]], lz_in.at[dz - 1], place)
    fin = lx_own[yl, yh, x, z]
    wait_bytes(recv_sem.at[RS_LZ], lz_in)
    for dz in range(Z - 1):
        fin = fin + lz_in[dz].astype(F32)
    out_ref[...] = fin

    wait_bytes(send_sem.at[GEO_S], geo_s.at[pl.ds(1, n_xy - 1)])
    wait_bytes(send_sem.at[GEO_T], geo_t.at[pl.ds(1, n_zc - 1)])
    wait_bytes(send_sem.at[RS_AMP], amp_in)
    wait_bytes(send_sem.at[AG_Z], amp.at[0, 0, 0, pl.ds(0, Z - 1)])
    wait_bytes(send_sem.at[AG_XY], kmat.at[0, pl.ds(0, (n_xy - 1) * mb * CW // (2 * PB)), :])
    wait_bytes(send_sem.at[AG_C], mine)
    wait_bytes(vsend_sem.at[0], vels.at[pl.ds(1, n_xy - 1)])
    wait_bytes(send_sem.at[RS_PZ], pz_in)
    wait_bytes(send_sem.at[RS_LXY], lx_in)
    wait_bytes(send_sem.at[RS_LZ], lz_in)


def solution(mesh):
    Z = mesh.shape["blk"] // YL
    YH = mesh.shape["tgt"] // 2
    X = mesh.shape["sec"]
    Y = YH * YL
    n_xy, n_zc, n_blk = X * Y, 2 * Z, YL * Z
    mb = Z * RW

    def on_device(modal_loads, receptance, shapes, coupling, panel_coords, panel_areas):
        KB = shapes.shape[1]
        dma = pltpu.SemaphoreType.DMA
        scratch = [
            pltpu.VMEM((n_xy, 8, PB), F32),
            pltpu.VMEM((n_zc, 8, PB), F32),
            pltpu.VMEM((3, n_zc * PB, PB), F32),
            pltpu.VMEM((PB, PB), F32),
            pltpu.VMEM((n_xy, n_zc * PB, 2 * PB), BF16),
            pltpu.VMEM((n_zc * PB, CW), F32),
            pltpu.VMEM((n_blk, RW, CW), F32),
            pltpu.VMEM((n_blk, RW, CW), BF16),
            pltpu.VMEM((n_blk - 1, RW, CW), BF16),
            pltpu.VMEM((YH, 2, X * YL, Z, RW, CW), BF16),
            pltpu.VMEM((n_xy, PB, CW), BF16),
            pltpu.VMEM((2 * PB, CW), BF16),
            pltpu.VMEM((Z, PB, CW), BF16),
            pltpu.VMEM((Z, PB, CW), BF16),
            pltpu.VMEM((Z - 1, PB, CW), BF16),
            pltpu.VMEM((KB, mb, PB), BF16),
            pltpu.SMEM((n_blk * YH,), jnp.int32),
            pltpu.VMEM((KB + 1, 2, X, RW, CW), BF16),
            pltpu.VMEM((n_blk * YH, X, RW, CW), BF16),
            pltpu.VMEM((n_blk * YH, X, RW, CW), BF16),
            pltpu.VMEM((YL, YH, X, Z, RW, CW), BF16),
            pltpu.VMEM((n_xy - 1, Z, RW, CW), BF16),
            pltpu.VMEM((YL, YH, X, Z, RW, CW), F32),
            pltpu.VMEM((Z, RW, CW), BF16),
            pltpu.VMEM((Z - 1, RW, CW), BF16),
            dma((11,)),
            dma((11,)),
            dma((1,)),
            dma((n_xy - 1,)),
        ]
        vmem = pl.BlockSpec(memory_space=pltpu.VMEM)
        new_loads, pressure = pl.pallas_call(
            functools.partial(kernel, (X, YH, Z, KB)),
            out_shape=(
                jax.ShapeDtypeStruct((RW, CW), F32),
                jax.ShapeDtypeStruct((PB, CW), BF16),
            ),
            in_specs=[vmem, vmem, vmem, pl.BlockSpec(memory_space=pltpu.SMEM), vmem, vmem],
            out_specs=(vmem, vmem),
            scratch_shapes=scratch,
            compiler_params=pltpu.CompilerParams(
                collective_id=0,
                has_side_effects=True,
                vmem_limit_bytes=58 * 1024 * 1024,
            ),
        )(
            modal_loads,
            receptance,
            jnp.transpose(shapes, (1, 0, 2)),
            coupling,
            panel_coords,
            panel_areas.reshape(1, PB),
        )
        return new_loads, pressure

    owned = ("blk", "tgt", "sec")
    in_specs = (
        P("blk", None),
        P(None, ("tgt", "sec"), "blk"),
        P(owned, None, None),
        P(owned, None),
        P(None, owned),
        P(owned),
    )
    return jax.shard_map(
        on_device,
        mesh=mesh,
        in_specs=in_specs,
        out_specs=(P(owned, None), P(owned, None)),
        check_vma=False,
    )
```

```python
import functools
import math

import jax
import jax.numpy as jnp
from jax import lax
from jax.experimental import pallas as pl
from jax.experimental.pallas import tpu as pltpu
from jax.sharding import PartitionSpec as P

MESH = pl.DeviceIdType.MESH
F32 = jnp.float32
BF16 = jnp.bfloat16

WAVE = 40.0
YL = 2
PB = 128
CW = 128
RW = 16
ROWS = 128

CUTS = (0, 3, 5, 7, 9, 11, 12, 14)

SIN = (4.442879567546083, -7.307816684491776, 3.5977741780871795, -0.7911993921612632)
COS = (1.4142040148090755, -6.977637323456285, 5.715187874756681, -1.7282138922234693)

GEO_S, GEO_T, RS_AMP, AG_Z, AG_C, RS_PZ, RS_LXY, RS_LZ, AG_XY, VEL, RS_PC, RS_LC, N_SEM = (
    0, 1, 2, 3, 4, 5, 6, 7, 8, 12, 16, 20, 24,
)


def horner(coefs, u):
    acc = u * coefs[-1] + coefs[-2]
    for value in coefs[-3::-1]:
        acc = acc * u + value
    return acc


def turn_rows(value):
    n = value.shape[1]
    return jnp.transpose(jnp.broadcast_to(value, (n, n)))


def rotated(value):
    half = value.shape[1] // 2
    turned = pltpu.roll(value, half, 1)
    lane = lax.broadcasted_iota(jnp.int32, value.shape, 1)
    return jnp.where(lane < half, -turned, turned)


def near(d, n):
    return min(d, n - d)


def kernel(
    dims,
    loads_ref,
    rec_ref,
    shp_ref,
    cpl_ref,
    crd_ref,
    area_ref,
    out_ref,
    prs_ref,
    geo_s,
    geo_t,
    tgt_b,
    area_b,
    kmat,
    acc,
    part,
    part_h,
    amp_in,
    amp,
    vels,
    w_ref,
    p_out,
    pc_in,
    pz_out,
    pz_in,
    shp_f,
    shp_k,
    shp_t,
    inv,
    cbuf,
    lc_out,
    lc_in,
    lx_out,
    lx_in,
    lx_own,
    lz_out,
    lz_in,
    send_sem,
    recv_sem,
):
    X, YH, Z, KB = dims
    Y = YH * YL
    n_xy, n_zc, n_blk = X * Y, 2 * Z, YL * Z
    mb = Z * RW
    total_panels = float(PB * 2 * X * Y * Z)

    blk, tgt, sec = lax.axis_index("blk"), lax.axis_index("tgt"), lax.axis_index("sec")
    yl, z = lax.div(blk, Z), lax.rem(blk, Z)
    yh, core = lax.div(tgt, 2), lax.rem(tgt, 2)
    x = sec
    y = yh * YL + yl

    def device(x_, y_, z_, c_):
        return (lax.rem(y_, YL) * Z + z_, lax.div(y_, YL) * 2 + c_, x_)

    def shifted(dx=0, dy=0, dz=0, dc=0):
        return (
            lax.rem(x + dx, X),
            lax.rem(y + dy, Y),
            lax.rem(z + dz, Z),
            lax.rem(core + dc, 2),
        )

    xy_steps = sorted(((q % X, q // X) for q in range(n_xy)), key=lambda s: near(s[0], X) + near(s[1], Y))
    z_steps = sorted(range(Z), key=lambda q: -near(q, Z))
    zc_steps = [(dc, dz) for dc in (1, 0) for dz in z_steps]
    y_steps = sorted(range(Y), key=lambda q: -near(q, Y))
    blk_steps = sorted(
        ((dl, dz) for dl in range(YL) for dz in range(Z) if dl or dz), key=lambda s: -s[0] - near(s[1], Z)
    )
    groups = [range(n_xy * g // 4, n_xy * (g + 1) // 4) for g in range(4)]

    def yl_place(dl, dz):
        y_ = yh * YL + lax.rem(yl + dl, YL)
        return (x, y_, lax.rem(z + dz, Z), core)

    def send(send_s, recv_s, src, dst, place):
        pltpu.make_async_remote_copy(
            src_ref=src,
            dst_ref=dst,
            send_sem=send_sem.at[send_s],
            recv_sem=recv_sem.at[recv_s],
            device_id=device(*place),
            device_id_type=MESH,
        ).start()

    def wait_bytes(sem, ref):
        pltpu.make_async_copy(ref, ref, sem).wait()

    unfinished = []

    def finish():
        for phase, ref in unfinished:
            wait_bytes(send_sem.at[phase], ref)

    barrier = pltpu.get_barrier_semaphore()
    places = [shifted(dx=dx, dy=dy) for dx, dy in reversed(xy_steps[1:])]
    places += [shifted(dz=dz, dc=dc) for dc, dz in zc_steps[:-1]]
    places += [yl_place(dl, dz) for dl, dz in blk_steps if dl and dz]
    for place in places:
        pl.semaphore_signal(barrier, inc=1, device_id=device(*place), device_id_type=MESH)

    half_scale = 0.5 * WAVE / math.pi
    geo_s[0, 0:3, :] = crd_ref[...] * half_scale
    geo_s[0, 3:4, :] = area_ref[...] * (half_scale * half_scale / total_panels)
    geo_s[0, 4:8, :] = jnp.zeros((4, PB), F32)
    geo_t[n_zc - 1, :, :] = geo_s[0, :, :]
    loads = loads_ref[...]
    loads_rot = rotated(loads.astype(F32)).astype(BF16)
    psum = jnp.dot(rec_ref[0], loads, preferred_element_type=F32) + jnp.dot(
        rec_ref[1], loads_rot, preferred_element_type=F32
    )
    part[...] = psum.reshape(n_blk, RW, CW)
    part_h[...] = psum.astype(BF16).reshape(n_blk, RW, CW)

    pl.semaphore_wait(barrier, len(places))

    for q, (dl, dz) in enumerate(blk_steps):
        place = yl_place(dl, dz)
        owner = lax.rem(place[1], YL) * Z + place[2]
        send(RS_AMP, RS_AMP, part_h.at[owner], amp_in.at[q], place)
    for n in range(1, n_xy):
        dx, dy = xy_steps[n]
        send(GEO_S, GEO_S, geo_s.at[0], geo_s.at[n], shifted(dx=dx, dy=dy))
    for t in range(n_zc - 1):
        dc, dz = zc_steps[t]
        send(GEO_T, GEO_T, geo_t.at[n_zc - 1], geo_t.at[t], shifted(dz=dz, dc=dc))
    unfinished.append((GEO_S, geo_s.at[pl.ds(1, n_xy - 1)]))
    unfinished.append((GEO_T, geo_t.at[pl.ds(1, n_zc - 1)]))
    unfinished.append((RS_AMP, amp_in))

    area_b[...] = turn_rows(area_ref[...])
    shp_f[...] = shp_ref[...].astype(F32).reshape(PB * KB, mb)
    for k in range(KB):
        block = shp_f[pl.ds(k, PB, stride=KB), :]
        shp_k[k] = block.astype(BF16)
        shp_t[k] = jnp.transpose(block).astype(BF16)
    cbuf[KB] = jnp.zeros((2, X, RW, CW), BF16)

    def fill_inv(j, carry):
        found = jnp.int32(KB)
        for k in range(KB):
            found = jnp.where(cpl_ref[0, k] == j, jnp.int32(k), found)
        inv[j] = found
        return carry

    lax.fori_loop(0, n_blk * YH, fill_inv, 0)

    wait_bytes(recv_sem.at[GEO_T], geo_t.at[pl.ds(1, n_zc - 1)])

    def turn_step(slot, carry):
        rows = pl.ds(pl.multiple_of(slot * PB, PB), PB)
        for axis in range(3):
            tgt_b[axis, rows, :] = turn_rows(geo_t[slot, axis : axis + 1, :])
        return carry

    lax.fori_loop(0, n_zc, turn_step, 0)
    wait_bytes(recv_sem.at[GEO_S], geo_s.at[pl.ds(1, n_xy - 1)])

    steps = n_zc * PB // ROWS

    def kernel_chunks(lo, hi):
        def chunk(d, carry):
            shape = (ROWS, PB)
            sx = jnp.broadcast_to(geo_s[d, 0:1, :], shape)
            sy = jnp.broadcast_to(geo_s[d, 1:2, :], shape)
            sz = jnp.broadcast_to(geo_s[d, 2:3, :], shape)
            sa = jnp.broadcast_to(geo_s[d, 3:4, :], shape)

            def rows_step(i, inner):
                rows = pl.ds(pl.multiple_of(i * ROWS, ROWS), ROWS)
                dx = tgt_b[0, rows, :] - sx
                dy = tgt_b[1, rows, :] - sy
                dz = tgt_b[2, rows, :] - sz
                d2 = dx * dx + dy * dy + dz * dz + sa
                r = lax.rsqrt(d2)
                h = d2 * r
                f = h - jnp.round(h)
                u = f * f
                s = horner(SIN, u) * f
                c = horner(COS, u)
                rs = r * s
                kmat[d, rows, 0:PB] = (r - rs * s).astype(BF16)
                kmat[d, rows, PB : 2 * PB] = (rs * c).astype(BF16)
                return inner

            return lax.fori_loop(0, steps, rows_step, carry)

        lax.fori_loop(lo, hi, chunk, 0)

    cuts = [round(n_xy * part_of / 16) for part_of in CUTS]

    kernel_chunks(cuts[0], cuts[1])

    wait_bytes(recv_sem.at[RS_AMP], amp_in)
    asum = part[blk]
    for q in range(n_blk - 1):
        asum = asum + amp_in[q].astype(F32)
    xl = x * YL + yl
    amp[yh, core, xl, z] = asum.astype(BF16)
    for dz in z_steps[:-1]:
        mine = amp.at[yh, core, xl, z]
        send(AG_Z, AG_Z, mine, mine, shifted(dz=dz))
    seven = amp.at[0, 0, 0, pl.ds(0, Z - 1)]
    unfinished.append((AG_Z, seven))

    kernel_chunks(cuts[1], cuts[2])
    wait_bytes(recv_sem.at[AG_Z], seven)
    mine = amp.at[yh, core, xl]
    for g, group in enumerate(groups):
        for n in group:
            dx, dy = xy_steps[n]
            if n:
                send(AG_XY, AG_XY + g, mine, mine, shifted(dx=dx, dy=dy))
    unfinished.append((AG_XY, vels.at[pl.ds(1, n_xy - 1), pl.ds(0, mb)]))
    send(AG_C, AG_C, mine, mine, shifted(dc=1))

    for g, group in enumerate(groups):
        kernel_chunks(cuts[2 + g], cuts[3 + g])
        rest = [n for n in group if n]
        if not rest:
            continue
        wait_bytes(recv_sem.at[AG_XY + g], vels.at[pl.ds(1, len(rest)), pl.ds(0, mb)])
        for n in rest:
            dx, dy = xy_steps[n]
            sx, sy = lax.rem(x + X - dx, X), lax.rem(y + Y - dy, Y)
            theirs = amp.at[lax.div(sy, YL), core, sx * YL + lax.rem(sy, YL)]
            send(AG_C, AG_C, theirs, theirs, shifted(dc=1))
    half_amp = amp.at[:, 0]
    unfinished.append((AG_C, half_amp))
    kernel_chunks(cuts[6], cuts[7])
    wait_bytes(recv_sem.at[AG_C], half_amp)

    vel = jnp.zeros((PB, CW), F32)
    for k in range(KB):
        j = cpl_ref[0, k]
        jl = lax.rem(j, X * YL)
        jc = lax.rem(lax.div(j, X * YL), 2)
        jh = lax.div(j, X * YL * 2)
        block = amp[jh, jc, jl].reshape(mb, CW)
        vel = vel + jnp.dot(shp_k[k], block, preferred_element_type=F32)
    vels[0] = (vel * area_b[...] * (half_scale / math.sqrt(total_panels))).astype(BF16)
    for g, group in enumerate(groups):
        for n in group:
            dx, dy = xy_steps[n]
            if n:
                send(VEL, VEL + g, vels.at[0], vels.at[n], shifted(dx=dx, dy=dy))
    unfinished.append((VEL, vels.at[pl.ds(1, n_xy - 1)]))
    kernel_chunks(cuts[7], n_xy)

    def weights(g):
        group = groups[g]
        rest = [n for n in group if n]
        if rest:
            wait_bytes(recv_sem.at[VEL + g], vels.at[pl.ds(rest[0], len(rest))])
        for n in group:
            value = vels[n]
            w_ref[n, 0:PB, :] = value
            w_ref[n, PB : 2 * PB, :] = rotated(value.astype(F32)).astype(BF16)

    def products(g, rows):
        total = None
        for n in groups[g]:
            term = jnp.dot(kmat[n, rows, :], w_ref[n], preferred_element_type=F32)
            total = term if total is None else total + term
        return total

    mm_rows = min(512, n_zc * PB)
    for g in range(3):
        weights(g)

        def mm_step(i, carry):
            rows = pl.ds(pl.multiple_of(i * mm_rows, mm_rows), mm_rows)
            prod = products(g, rows)
            acc[rows, :] = prod if g == 0 else acc[rows, :] + prod
            return carry

        lax.fori_loop(0, n_zc * PB // mm_rows, mm_step, 0)

    weights(3)
    pair = 2
    n_pair = Z // pair
    for i in range(n_pair):
        rows = slice(i * pair * PB, (i + 1) * pair * PB)
        value = acc[rows, :] + products(3, rows)
        p_out[i] = value.astype(BF16).reshape(pair, PB, CW)
        send(RS_PC, RS_PC + i, p_out.at[i], pc_in.at[i], shifted(dc=1))
    unfinished.append((RS_PC, p_out))
    total = None
    for i in range(n_pair):
        rows = slice((n_pair + i) * pair * PB, (n_pair + i + 1) * pair * PB)
        value = acc[rows, :] + products(3, rows)
        wait_bytes(recv_sem.at[RS_PC + i], pc_in.at[i])
        value = value + pc_in[i].astype(F32).reshape(pair * PB, CW)
        for h in range(pair):
            t = i * pair + h
            part_p = value[h * PB : (h + 1) * PB]
            if t == Z - 1:
                total = part_p
            else:
                pz_out[t] = part_p.astype(BF16)
                send(RS_PZ, RS_PZ, pz_out.at[t], pz_in.at[t], shifted(dz=Z - z_steps[t]))
    unfinished.append((RS_PZ, pz_in))
    wait_bytes(recv_sem.at[RS_PZ], pz_in)
    for t in range(Z - 1):
        total = total + pz_in[t].astype(F32)
    pressure = total.astype(BF16)
    prs_ref[...] = pressure
    weighted = (area_b[...] * pressure.astype(F32)).astype(BF16)

    for k in range(KB):
        cbuf[k] = (
            jnp.dot(shp_t[k], weighted, preferred_element_type=F32)
            .astype(BF16)
            .reshape(2, X, RW, CW)
        )
    other = 1 - core
    for n, dy in enumerate(y_steps):
        y_ = lax.rem(y + dy, Y)
        first = lax.rem(y_, YL) * (Z * YH) + lax.div(y_, YL)
        for zz in range(Z):
            lc_out[n, zz] = cbuf[inv[first + zz * YH], other]
        send(RS_LC, RS_LC + n, lc_out.at[n], lc_in.at[n], shifted(dc=1))
    unfinished.append((RS_LC, lc_out))
    lx_slot = 0
    for n, dy in enumerate(y_steps):
        y_ = lax.rem(y + dy, Y)
        first = lax.rem(y_, YL) * (Z * YH) + lax.div(y_, YL)
        wait_bytes(recv_sem.at[RS_LC + n], lc_in.at[n])
        for zz in range(Z):
            both = cbuf[inv[first + zz * YH], core].astype(F32) + lc_in[n, zz].astype(F32)
            for xx in range(X):
                lx_out[n, xx, zz] = both[xx].astype(BF16)
                if dy == 0:
                    lx_own[xx, zz] = both[xx]
        for dx in sorted(range(X), key=lambda q: -near(q, X)):
            if dx or dy:
                place = shifted(dx=dx, dy=dy)
                send(RS_LXY, RS_LXY, lx_out.at[n, place[0]], lx_in.at[lx_slot], place)
                lx_slot += 1
    unfinished.append((RS_LXY, lx_in))
    wait_bytes(recv_sem.at[RS_LXY], lx_in)
    lsum = lx_own[x]
    for q in range(n_xy - 1):
        lsum = lsum + lx_in[q].astype(F32)
    lx_own[x] = lsum
    lz_out[...] = lsum.astype(BF16)
    for t, dz in enumerate(z_steps[:-1]):
        place = shifted(dz=dz)
        send(RS_LZ, RS_LZ, lz_out.at[place[2]], lz_in.at[t], place)
    unfinished.append((RS_LZ, lz_in))
    fin = lx_own[x, z]
    wait_bytes(recv_sem.at[RS_LZ], lz_in)
    for t in range(Z - 1):
        fin = fin + lz_in[t].astype(F32)
    out_ref[...] = fin
    finish()


def copy_kernel(a_ref, b_ref, c_ref, d_ref):
    c_ref[...] = a_ref[...]
    d_ref[...] = b_ref[...]


def solution(mesh):
    Z = mesh.shape["blk"] // YL
    YH = mesh.shape["tgt"] // 2
    X = mesh.shape["sec"]
    Y = YH * YL
    n_xy, n_zc, n_blk = X * Y, 2 * Z, YL * Z
    mb = Z * RW

    def on_device(modal_loads, receptance, shapes, coupling, panel_coords, panel_areas):
        KB = shapes.shape[1]
        scratch = [
            pltpu.VMEM((n_xy, 8, PB), F32),
            pltpu.VMEM((n_zc, 8, PB), F32),
            pltpu.VMEM((3, n_zc * PB, PB), F32),
            pltpu.VMEM((PB, PB), F32),
            pltpu.VMEM((n_xy, n_zc * PB, 2 * PB), BF16),
            pltpu.VMEM((n_zc * PB, CW), F32),
            pltpu.VMEM((n_blk, RW, CW), F32),
            pltpu.VMEM((n_blk, RW, CW), BF16),
            pltpu.VMEM((n_blk - 1, RW, CW), BF16),
            pltpu.VMEM((YH, 2, X * YL, Z, RW, CW), BF16),
            pltpu.VMEM((n_xy, PB, CW), BF16),
            pltpu.VMEM((n_xy, 2 * PB, CW), BF16),
            pltpu.VMEM((Z // 2, 2, PB, CW), BF16),
            pltpu.VMEM((Z // 2, 2, PB, CW), BF16),
            pltpu.VMEM((Z - 1, PB, CW), BF16),
            pltpu.VMEM((Z - 1, PB, CW), BF16),
            pltpu.VMEM((PB * KB, mb), F32),
            pltpu.VMEM((KB, PB, mb), BF16),
            pltpu.VMEM((KB, mb, PB), BF16),
            pltpu.SMEM((n_blk * YH,), jnp.int32),
            pltpu.VMEM((KB + 1, 2, X, RW, CW), BF16),
            pltpu.VMEM((Y, Z, X, RW, CW), BF16),
            pltpu.VMEM((Y, Z, X, RW, CW), BF16),
            pltpu.VMEM((Y, X, Z, RW, CW), BF16),
            pltpu.VMEM((n_xy - 1, Z, RW, CW), BF16),
            pltpu.VMEM((X, Z, RW, CW), F32),
            pltpu.VMEM((Z, RW, CW), BF16),
            pltpu.VMEM((Z - 1, RW, CW), BF16),
            pltpu.SemaphoreType.DMA((N_SEM,)),
            pltpu.SemaphoreType.DMA((N_SEM,)),
        ]
        vmem = pl.BlockSpec(memory_space=pltpu.VMEM)
        outs = (
            jax.ShapeDtypeStruct((RW, CW), F32),
            jax.ShapeDtypeStruct((PB, CW), BF16),
        )
        results = pl.pallas_call(
            functools.partial(kernel, (X, YH, Z, KB)),
            out_shape=outs,
            in_specs=[vmem, vmem, vmem, pl.BlockSpec(memory_space=pltpu.SMEM), vmem, vmem],
            out_specs=(vmem, vmem),
            scratch_shapes=scratch,
            compiler_params=pltpu.CompilerParams(
                collective_id=0,
                has_side_effects=True,
                vmem_limit_bytes=58 * 1024 * 1024,
            ),
        )(
            modal_loads,
            receptance,
            shapes,
            coupling,
            panel_coords,
            panel_areas.reshape(1, PB),
        )
        return pl.pallas_call(
            copy_kernel,
            out_shape=outs,
            in_specs=[vmem, vmem],
            out_specs=(vmem, vmem),
        )(*results)

    owned = ("blk", "tgt", "sec")
    in_specs = (
        P("blk", None),
        P(None, ("tgt", "sec"), "blk"),
        P(owned, None, None),
        P(owned, None),
        P(None, owned),
        P(owned),
    )
    return jax.shard_map(
        on_device,
        mesh=mesh,
        in_specs=in_specs,
        out_specs=(P(owned, None), P(owned, None)),
        check_vma=False,
    )
```

```python
import functools
import math

import jax
import jax.numpy as jnp
from jax import lax
from jax.experimental import pallas as pl
from jax.experimental.pallas import tpu as pltpu
from jax.sharding import PartitionSpec as P

MESH = pl.DeviceIdType.MESH
F32 = jnp.float32
BF16 = jnp.bfloat16

WAVE = 40.0
YL = 2
PB = 128
CW = 128
RW = 16
ROWS = 128

CUTS = (2, 4, 7, 9, 10, 11, 12, 13, 16)

SIN = (4.442879567546083, -7.307816684491776, 3.5977741780871795, -0.7911993921612632)
COS = (1.4142040148090755, -6.977637323456285, 5.715187874756681, -1.7282138922234693)

GEO_S, GEO_T, RS_AMP, AG_Z, AG_C, RS_PZ, RS_LXY, RS_LZ, AG_XY, VEL, RS_PC, RS_LC, INP, N_SEM = (
    0, 1, 2, 3, 4, 5, 6, 7, 8, 12, 16, 20, 24, 30,
)


def horner(coefs, u):
    acc = u * coefs[-1] + coefs[-2]
    for value in coefs[-3::-1]:
        acc = acc * u + value
    return acc


def turn_rows(value):
    n = value.shape[1]
    return jnp.transpose(jnp.broadcast_to(value, (n, n)))


def rotated(value):
    half = value.shape[1] // 2
    turned = pltpu.roll(value, half, 1)
    lane = lax.broadcasted_iota(jnp.int32, value.shape, 1)
    return jnp.where(lane < half, -turned, turned)


def near(d, n):
    return min(d, n - d)


def kernel(
    dims,
    loads_hbm,
    rec_hbm,
    shp_hbm,
    cpl_hbm,
    crd_hbm,
    area_hbm,
    out_ref,
    prs_ref,
    loads_ref,
    rec_ref,
    shp_ref,
    cpl_ref,
    crd_ref,
    area_ref,
    geo_s,
    geo_t,
    tgt_b,
    area_b,
    kmat,
    acc,
    part,
    part_h,
    amp_in,
    amp,
    vels,
    w_ref,
    p_out,
    pc_in,
    pz_out,
    pz_in,
    shp_f,
    shp_k,
    shp_t,
    inv,
    cbuf,
    lc_out,
    lc_in,
    lx_out,
    lx_in,
    lx_own,
    lz_out,
    lz_in,
    send_sem,
    recv_sem,
):
    X, YH, Z, KB = dims
    Y = YH * YL
    n_xy, n_zc, n_blk = X * Y, 2 * Z, YL * Z
    mb = Z * RW
    total_panels = float(PB * 2 * X * Y * Z)

    blk, tgt, sec = lax.axis_index("blk"), lax.axis_index("tgt"), lax.axis_index("sec")
    yl, z = lax.div(blk, Z), lax.rem(blk, Z)
    yh, core = lax.div(tgt, 2), lax.rem(tgt, 2)
    x = sec
    y = yh * YL + yl

    def device(x_, y_, z_, c_):
        return (lax.rem(y_, YL) * Z + z_, lax.div(y_, YL) * 2 + c_, x_)

    def shifted(dx=0, dy=0, dz=0, dc=0):
        return (
            lax.rem(x + dx, X),
            lax.rem(y + dy, Y),
            lax.rem(z + dz, Z),
            lax.rem(core + dc, 2),
        )

    xy_steps = sorted(((q % X, q // X) for q in range(n_xy)), key=lambda s: near(s[0], X) + near(s[1], Y))
    z_steps = sorted(range(Z), key=lambda q: -near(q, Z))
    zc_steps = [(dc, dz) for dc in (1, 0) for dz in z_steps]
    y_steps = sorted(range(Y), key=lambda q: -near(q, Y))
    blk_steps = sorted(
        ((dl, dz) for dl in range(YL) for dz in range(Z) if dl or dz), key=lambda s: -s[0] - near(s[1], Z)
    )
    edges = (0, min(5, n_xy - 2), min(11, n_xy - 1), n_xy)
    groups = [range(lo, hi) for lo, hi in zip(edges, edges[1:])]

    def yl_place(dl, dz):
        y_ = yh * YL + lax.rem(yl + dl, YL)
        return (x, y_, lax.rem(z + dz, Z), core)

    def send(send_s, recv_s, src, dst, place):
        pltpu.make_async_remote_copy(
            src_ref=src,
            dst_ref=dst,
            send_sem=send_sem.at[send_s],
            recv_sem=recv_sem.at[recv_s],
            device_id=device(*place),
            device_id_type=MESH,
        ).start()

    def wait_bytes(sem, ref):
        pltpu.make_async_copy(ref, ref, sem).wait()

    unfinished = []

    def finish():
        for phase, ref in unfinished:
            wait_bytes(send_sem.at[phase], ref)

    barrier = pltpu.get_barrier_semaphore()
    places = [shifted(dx=dx, dy=dy) for dx, dy in reversed(xy_steps[1:])]
    places += [shifted(dz=dz, dc=dc) for dc, dz in zc_steps[:-1]]
    places += [yl_place(dl, dz) for dl, dz in blk_steps if dl and dz]
    for place in places:
        pl.semaphore_signal(barrier, inc=1, device_id=device(*place), device_id_type=MESH)

    inputs = [
        pltpu.make_async_copy(src, dst, recv_sem.at[INP + i])
        for i, (src, dst) in enumerate(
            (
                (crd_hbm, crd_ref),
                (area_hbm, area_ref),
                (loads_hbm, loads_ref),
                (rec_hbm, rec_ref),
                (shp_hbm, shp_ref),
                (cpl_hbm, cpl_ref),
            )
        )
    ]
    for copy in inputs:
        copy.start()
    inputs[0].wait()
    inputs[1].wait()
    half_scale = 0.5 * WAVE / math.pi
    geo_s[0, 0:3, :] = crd_ref[...] * half_scale
    geo_s[0, 3:4, :] = area_ref[...] * (half_scale * half_scale / total_panels)
    geo_t[n_zc - 1, :, :] = geo_s[0, :, :]
    inputs[2].wait()
    inputs[3].wait()
    loads = loads_ref[...]
    loads_rot = rotated(loads.astype(F32)).astype(BF16)
    psum = jnp.dot(rec_ref[0], loads, preferred_element_type=F32) + jnp.dot(
        rec_ref[1], loads_rot, preferred_element_type=F32
    )
    part[...] = psum.reshape(n_blk, RW, CW)
    part_h[...] = psum.astype(BF16).reshape(n_blk, RW, CW)

    pl.semaphore_wait(barrier, len(places))

    for q, (dl, dz) in enumerate(blk_steps):
        place = yl_place(dl, dz)
        owner = lax.rem(place[1], YL) * Z + place[2]
        send(RS_AMP, RS_AMP, part_h.at[owner], amp_in.at[q], place)
    for n in range(1, n_xy):
        dx, dy = xy_steps[n]
        send(GEO_S, GEO_S, geo_s.at[0], geo_s.at[n], shifted(dx=dx, dy=dy))
    for t in range(n_zc - 1):
        dc, dz = zc_steps[t]
        send(GEO_T, GEO_T, geo_t.at[n_zc - 1], geo_t.at[t], shifted(dz=dz, dc=dc))
    unfinished.append((GEO_S, geo_s.at[pl.ds(1, n_xy - 1)]))
    unfinished.append((GEO_T, geo_t.at[pl.ds(1, n_zc - 1)]))
    unfinished.append((RS_AMP, amp_in))

    def prepare():
        inputs[4].wait()
        area_b[...] = turn_rows(area_ref[...])
        shp_f[...] = shp_ref[...].astype(F32).reshape(PB * KB, mb)
        for k in range(KB):
            block = shp_f[pl.ds(k, PB, stride=KB), :]
            shp_k[k] = block.astype(BF16)
            shp_t[k] = jnp.transpose(block).astype(BF16)
        cbuf[KB] = jnp.zeros((2, X, RW, CW), BF16)
        inputs[5].wait()

        def fill_inv(j, carry):
            found = jnp.int32(KB)
            for k in range(KB):
                found = jnp.where(cpl_ref[0, k] == j, jnp.int32(k), found)
            inv[j] = found
            return carry

        lax.fori_loop(0, n_blk * YH, fill_inv, 0)

    def turn_step(slot, carry):
        rows = pl.ds(pl.multiple_of(slot * PB, PB), PB)
        for axis in range(3):
            tgt_b[axis, rows, :] = turn_rows(geo_t[slot, axis : axis + 1, :])
        return carry

    steps = n_zc * PB // ROWS

    def kernel_chunks(lo, hi):
        def chunk(d, carry):
            shape = (ROWS, PB)
            sx = jnp.broadcast_to(geo_s[d, 0:1, :], shape)
            sy = jnp.broadcast_to(geo_s[d, 1:2, :], shape)
            sz = jnp.broadcast_to(geo_s[d, 2:3, :], shape)
            sa = jnp.broadcast_to(geo_s[d, 3:4, :], shape)

            def rows_step(i, inner):
                rows = pl.ds(pl.multiple_of(i * ROWS, ROWS), ROWS)
                dx = tgt_b[0, rows, :] - sx
                dy = tgt_b[1, rows, :] - sy
                dz = tgt_b[2, rows, :] - sz
                d2 = dx * dx + dy * dy + dz * dz + sa
                r = lax.rsqrt(d2)
                h = d2 * r
                f = h - jnp.round(h)
                u = f * f
                s = horner(SIN, u) * f
                c = horner(COS, u)
                rs = r * s
                kmat[d, rows, 0:PB] = (r - rs * s).astype(BF16)
                kmat[d, rows, PB : 2 * PB] = (rs * c).astype(BF16)
                return inner

            return lax.fori_loop(0, steps, rows_step, carry)

        lax.fori_loop(lo, hi, chunk, 0)

    cuts = [round(n_xy * part_of / 16) for part_of in CUTS]

    prepare()

    wait_bytes(recv_sem.at[RS_AMP], amp_in)
    asum = part[blk]
    for q in range(n_blk - 1):
        asum = asum + amp_in[q].astype(F32)
    xl = x * YL + yl
    amp[yh, core, xl, z] = asum.astype(BF16)
    for dz in z_steps[:-1]:
        mine = amp.at[yh, core, xl, z]
        send(AG_Z, AG_Z, mine, mine, shifted(dz=dz))
    seven = amp.at[0, 0, 0, pl.ds(0, Z - 1)]
    unfinished.append((AG_Z, seven))

    wait_bytes(recv_sem.at[GEO_T], geo_t.at[pl.ds(1, n_zc - 1)])
    lax.fori_loop(0, n_zc, turn_step, 0)
    wait_bytes(recv_sem.at[GEO_S], geo_s.at[pl.ds(1, n_xy - 1)])
    kernel_chunks(0, cuts[0])
    wait_bytes(recv_sem.at[AG_Z], seven)
    mine = amp.at[yh, core, xl]

    def send_block(g):
        for n in groups[g]:
            dx, dy = xy_steps[n]
            if n:
                send(AG_XY, AG_XY + g, mine, mine, shifted(dx=dx, dy=dy))

    send_block(2)
    send_block(1)
    send(AG_C, AG_C, mine, mine, shifted(dc=1))
    kernel_chunks(cuts[0], cuts[1])
    send_block(0)
    unfinished.append((AG_XY, vels.at[pl.ds(1, n_xy - 1), pl.ds(0, mb)]))

    for i, g in enumerate((2, 1, 0)):
        kernel_chunks(cuts[1 + i], cuts[2 + i])
        rest = [n for n in groups[g] if n]
        if not rest:
            continue
        wait_bytes(recv_sem.at[AG_XY + g], vels.at[pl.ds(1, len(rest)), pl.ds(0, mb)])
        for n in rest:
            dx, dy = xy_steps[n]
            sx, sy = lax.rem(x + X - dx, X), lax.rem(y + Y - dy, Y)
            theirs = amp.at[lax.div(sy, YL), core, sx * YL + lax.rem(sy, YL)]
            send(AG_C, AG_C, theirs, theirs, shifted(dc=1))
    half_amp = amp.at[:, 0]
    unfinished.append((AG_C, half_amp))
    kernel_chunks(cuts[4], cuts[5])
    wait_bytes(recv_sem.at[AG_C], half_amp)

    vel = jnp.zeros((PB, CW), F32)
    for k in range(KB):
        j = cpl_ref[0, k]
        jl = lax.rem(j, X * YL)
        jc = lax.rem(lax.div(j, X * YL), 2)
        jh = lax.div(j, X * YL * 2)
        block = amp[jh, jc, jl].reshape(mb, CW)
        vel = vel + jnp.dot(shp_k[k], block, preferred_element_type=F32)
    vels[0] = (vel * area_b[...] * (half_scale / math.sqrt(total_panels))).astype(BF16)
    for g, group in enumerate(groups):
        for n in group:
            dx, dy = xy_steps[n]
            if n:
                send(VEL, VEL + g, vels.at[0], vels.at[n], shifted(dx=dx, dy=dy))
        kernel_chunks(cuts[5 + g], cuts[6 + g])
    unfinished.append((VEL, vels.at[pl.ds(1, n_xy - 1)]))

    def weights(g):
        group = groups[g]
        rest = [n for n in group if n]
        if rest:
            wait_bytes(recv_sem.at[VEL + g], vels.at[pl.ds(rest[0], len(rest))])
        for n in group:
            value = vels[n]
            w_ref[n, 0:PB, :] = value
            w_ref[n, PB : 2 * PB, :] = rotated(value.astype(F32)).astype(BF16)

    def products(g, rows):
        total = None
        for n in groups[g]:
            term = jnp.dot(kmat[n, rows, :], w_ref[n], preferred_element_type=F32)
            total = term if total is None else total + term
        return total

    mm_rows = min(1024, n_zc * PB)
    last = len(groups) - 1
    for g in range(last):
        weights(g)

        def mm_step(i, carry):
            rows = pl.ds(pl.multiple_of(i * mm_rows, mm_rows), mm_rows)
            prod = products(g, rows)
            acc[rows, :] = prod if g == 0 else acc[rows, :] + prod
            return carry

        lax.fori_loop(0, n_zc * PB // mm_rows, mm_step, 0)

    weights(last)
    pair = 2
    n_pair = Z // pair

    def other_core(i):
        rows = pl.ds(pl.multiple_of(i * (pair * PB), pair * PB), pair * PB)
        value = acc[rows, :] + products(last, rows)
        p_out[i] = value.astype(BF16).reshape(pair, PB, CW)
        send(RS_PC, RS_PC + i, p_out.at[i], pc_in.at[i], shifted(dc=1))

    def this_core(i, final=False):
        rows = pl.ds(pl.multiple_of((n_pair + i) * (pair * PB), pair * PB), pair * PB)
        value = acc[rows, :] + products(last, rows)
        wait_bytes(recv_sem.at[RS_PC + i], pc_in.at[i])
        value = value + pc_in[i].astype(F32).reshape(pair * PB, CW)
        for h in range(pair):
            t = i * pair + h
            part_p = value[h * PB : (h + 1) * PB]
            if final and h == pair - 1:
                return part_p
            back = Z // 2 + i + 1 if h else Z // 2 - i
            pz_out[t] = part_p.astype(BF16)
            send(RS_PZ, RS_PZ, pz_out.at[t], pz_in.at[t], shifted(dz=back))

    def first_steps(i, carry):
        other_core(i)
        return carry

    def middle_steps(i, carry):
        other_core(i + ahead)
        this_core(i)
        return carry

    def later_steps(i, carry):
        this_core(i)
        return carry

    ahead = min(2, n_pair)
    lax.fori_loop(0, ahead, first_steps, 0)
    lax.fori_loop(0, n_pair - ahead, middle_steps, 0)
    lax.fori_loop(n_pair - ahead, n_pair - 1, later_steps, 0)
    total = this_core(n_pair - 1, final=True)
    unfinished.append((RS_PC, p_out))
    unfinished.append((RS_PZ, pz_in))
    wait_bytes(recv_sem.at[RS_PZ], pz_in)
    for t in range(Z - 1):
        total = total + pz_in[t].astype(F32)
    pressure = total.astype(BF16)
    prs_ref[...] = pressure
    weighted = (area_b[...] * pressure.astype(F32)).astype(BF16)

    for k in range(KB):
        cbuf[k] = (
            jnp.dot(shp_t[k], weighted, preferred_element_type=F32)
            .astype(BF16)
            .reshape(2, X, RW, CW)
        )
    other = 1 - core
    for n, dy in enumerate(y_steps):
        y_ = lax.rem(y + dy, Y)
        first = lax.rem(y_, YL) * (Z * YH) + lax.div(y_, YL)
        for zz in range(Z):
            lc_out[n, zz] = cbuf[inv[first + zz * YH], other]
        send(RS_LC, RS_LC + n, lc_out.at[n], lc_in.at[n], shifted(dc=1))
    unfinished.append((RS_LC, lc_out))
    lx_slot = 0
    for n, dy in enumerate(y_steps):
        y_ = lax.rem(y + dy, Y)
        first = lax.rem(y_, YL) * (Z * YH) + lax.div(y_, YL)
        wait_bytes(recv_sem.at[RS_LC + n], lc_in.at[n])
        for zz in range(Z):
            both = cbuf[inv[first + zz * YH], core].astype(F32) + lc_in[n, zz].astype(F32)
            for xx in range(X):
                lx_out[n, xx, zz] = both[xx].astype(BF16)
                if dy == 0:
                    lx_own[xx, zz] = both[xx]
        for dx in sorted(range(X), key=lambda q: -near(q, X)):
            if dx or dy:
                place = shifted(dx=dx, dy=dy)
                send(RS_LXY, RS_LXY, lx_out.at[n, place[0]], lx_in.at[lx_slot], place)
                lx_slot += 1
    unfinished.append((RS_LXY, lx_in))
    wait_bytes(recv_sem.at[RS_LXY], lx_in)
    lsum = lx_own[x]
    for q in range(n_xy - 1):
        lsum = lsum + lx_in[q].astype(F32)
    lx_own[x] = lsum
    lz_out[...] = lsum.astype(BF16)
    for t, dz in enumerate(z_steps[:-1]):
        place = shifted(dz=dz)
        send(RS_LZ, RS_LZ, lz_out.at[place[2]], lz_in.at[t], place)
    unfinished.append((RS_LZ, lz_in))
    fin = lx_own[x, z]
    wait_bytes(recv_sem.at[RS_LZ], lz_in)
    for t in range(Z - 1):
        fin = fin + lz_in[t].astype(F32)
    out_ref[...] = fin
    finish()


def copy_kernel(a_ref, b_ref, c_ref, d_ref):
    c_ref[...] = a_ref[...]
    d_ref[...] = b_ref[...]


def solution(mesh):
    Z = mesh.shape["blk"] // YL
    YH = mesh.shape["tgt"] // 2
    X = mesh.shape["sec"]
    Y = YH * YL
    n_xy, n_zc, n_blk = X * Y, 2 * Z, YL * Z
    mb = Z * RW

    def on_device(modal_loads, receptance, shapes, coupling, panel_coords, panel_areas):
        KB = shapes.shape[1]
        scratch = [
            pltpu.VMEM(modal_loads.shape, BF16),
            pltpu.VMEM(receptance.shape, BF16),
            pltpu.VMEM(shapes.shape, BF16),
            pltpu.SMEM(coupling.shape, jnp.int32),
            pltpu.VMEM(panel_coords.shape, F32),
            pltpu.VMEM((1, PB), F32),
            pltpu.VMEM((n_xy, 4, PB), F32),
            pltpu.VMEM((n_zc, 4, PB), F32),
            pltpu.VMEM((3, n_zc * PB, PB), F32),
            pltpu.VMEM((PB, PB), F32),
            pltpu.VMEM((n_xy, n_zc * PB, 2 * PB), BF16),
            pltpu.VMEM((n_zc * PB, CW), F32),
            pltpu.VMEM((n_blk, RW, CW), F32),
            pltpu.VMEM((n_blk, RW, CW), BF16),
            pltpu.VMEM((n_blk - 1, RW, CW), BF16),
            pltpu.VMEM((YH, 2, X * YL, Z, RW, CW), BF16),
            pltpu.VMEM((n_xy, PB, CW), BF16),
            pltpu.VMEM((n_xy, 2 * PB, CW), BF16),
            pltpu.VMEM((Z // 2, 2, PB, CW), BF16),
            pltpu.VMEM((Z // 2, 2, PB, CW), BF16),
            pltpu.VMEM((Z - 1, PB, CW), BF16),
            pltpu.VMEM((Z - 1, PB, CW), BF16),
            pltpu.VMEM((PB * KB, mb), F32),
            pltpu.VMEM((KB, PB, mb), BF16),
            pltpu.VMEM((KB, mb, PB), BF16),
            pltpu.SMEM((n_blk * YH,), jnp.int32),
            pltpu.VMEM((KB + 1, 2, X, RW, CW), BF16),
            pltpu.VMEM((Y, Z, X, RW, CW), BF16),
            pltpu.VMEM((Y, Z, X, RW, CW), BF16),
            pltpu.VMEM((Y, X, Z, RW, CW), BF16),
            pltpu.VMEM((n_xy - 1, Z, RW, CW), BF16),
            pltpu.VMEM((X, Z, RW, CW), F32),
            pltpu.VMEM((Z, RW, CW), BF16),
            pltpu.VMEM((Z - 1, RW, CW), BF16),
            pltpu.SemaphoreType.DMA((N_SEM,)),
            pltpu.SemaphoreType.DMA((N_SEM,)),
        ]
        vmem = pl.BlockSpec(memory_space=pltpu.VMEM)
        outs = (
            jax.ShapeDtypeStruct((RW, CW), F32),
            jax.ShapeDtypeStruct((PB, CW), BF16),
        )
        results = pl.pallas_call(
            functools.partial(kernel, (X, YH, Z, KB)),
            out_shape=outs,
            in_specs=[pl.BlockSpec(memory_space=pl.ANY)] * 6,
            out_specs=(vmem, vmem),
            scratch_shapes=scratch,
            compiler_params=pltpu.CompilerParams(
                collective_id=0,
                has_side_effects=True,
                vmem_limit_bytes=58 * 1024 * 1024,
            ),
        )(
            modal_loads,
            receptance,
            shapes,
            coupling,
            panel_coords,
            panel_areas.reshape(1, PB),
        )
        return pl.pallas_call(
            copy_kernel,
            out_shape=outs,
            in_specs=[vmem, vmem],
            out_specs=(vmem, vmem),
        )(*results)

    owned = ("blk", "tgt", "sec")
    in_specs = (
        P("blk", None),
        P(None, ("tgt", "sec"), "blk"),
        P(owned, None, None),
        P(owned, None),
        P(None, owned),
        P(owned),
    )
    return jax.shard_map(
        on_device,
        mesh=mesh,
        in_specs=in_specs,
        out_specs=(P(owned, None), P(owned, None)),
        check_vma=False,
    )
```

```python
import functools
import math

import jax
import jax.numpy as jnp
from jax import lax
from jax.experimental import pallas as pl
from jax.experimental.pallas import tpu as pltpu
from jax.sharding import PartitionSpec as P

MESH = pl.DeviceIdType.MESH
F32 = jnp.float32
BF16 = jnp.bfloat16

WAVE = 40.0
YL = 2
PB = 128
CW = 128
RW = 16
ROWS = 256

CUTS = (2, 4, 7, 9, 10, 11)

SIN = (4.442879567546083, -7.307816684491776, 3.5977741780871795, -0.7911993921612632)
COS = (1.4142040148090755, -6.977637323456285, 5.715187874756681, -1.7282138922234693)

GEO_S, GEO_T, RS_AMP, AG_Z, AG_C, RS_PZ, RS_LXY, RS_LZ, AG_XY, VEL, RS_PC, RS_LC, INP, N_SEM = (
    0, 1, 2, 3, 4, 5, 6, 7, 8, 12, 16, 20, 24, 30,
)


def horner(coefs, u):
    acc = u * coefs[-1] + coefs[-2]
    for value in coefs[-3::-1]:
        acc = acc * u + value
    return acc


def turn_rows(value):
    n = value.shape[1]
    return jnp.transpose(jnp.broadcast_to(value, (n, n)))


def rotated(value):
    half = value.shape[1] // 2
    turned = pltpu.roll(value, half, 1)
    lane = lax.broadcasted_iota(jnp.int32, value.shape, 1)
    return jnp.where(lane < half, -turned, turned)


def near(d, n):
    return min(d, n - d)


def kernel(
    dims,
    loads_hbm,
    rec_hbm,
    shp_hbm,
    cpl_hbm,
    crd_hbm,
    area_hbm,
    out_ref,
    prs_ref,
    loads_ref,
    rec_ref,
    shp_ref,
    cpl_ref,
    crd_ref,
    area_ref,
    geo_s,
    geo_t,
    tgt_b,
    area_b,
    kmat,
    acc,
    part,
    part_h,
    amp_in,
    amp,
    vels,
    w_ref,
    p_out,
    pc_in,
    pz_out,
    pz_in,
    shp_f,
    shp_k,
    shp_t,
    inv,
    cbuf,
    lc_out,
    lc_in,
    lx_out,
    lx_in,
    lx_own,
    lz_out,
    lz_in,
    send_sem,
    recv_sem,
):
    X, YH, Z, KB = dims
    Y = YH * YL
    n_xy, n_zc, n_blk = X * Y, 2 * Z, YL * Z
    mb = Z * RW
    total_panels = float(PB * 2 * X * Y * Z)

    blk, tgt, sec = lax.axis_index("blk"), lax.axis_index("tgt"), lax.axis_index("sec")
    yl, z = lax.div(blk, Z), lax.rem(blk, Z)
    yh, core = lax.div(tgt, 2), lax.rem(tgt, 2)
    x = sec
    y = yh * YL + yl

    def device(x_, y_, z_, c_):
        return (lax.rem(y_, YL) * Z + z_, lax.div(y_, YL) * 2 + c_, x_)

    def shifted(dx=0, dy=0, dz=0, dc=0):
        return (
            lax.rem(x + dx, X),
            lax.rem(y + dy, Y),
            lax.rem(z + dz, Z),
            lax.rem(core + dc, 2),
        )

    xy_steps = sorted(((q % X, q // X) for q in range(n_xy)), key=lambda s: near(s[0], X) + near(s[1], Y))
    z_steps = sorted(range(Z), key=lambda q: -near(q, Z))
    zc_steps = [(dc, dz) for dc in (1, 0) for dz in z_steps]
    y_steps = sorted(range(Y), key=lambda q: -near(q, Y))
    blk_steps = sorted(
        ((dl, dz) for dl in range(YL) for dz in range(Z) if dl or dz), key=lambda s: -s[0] - near(s[1], Z)
    )
    edges = (0, min(5, n_xy - 2), min(11, n_xy - 1), n_xy)
    used = (0, min(5, n_xy - 2), min(13, n_xy - 1), n_xy)
    groups = [range(lo, hi) for lo, hi in zip(edges, edges[1:])]
    batches = [range(lo, hi) for lo, hi in zip(used, used[1:])]

    def yl_place(dl, dz):
        y_ = yh * YL + lax.rem(yl + dl, YL)
        return (x, y_, lax.rem(z + dz, Z), core)

    def send(send_s, recv_s, src, dst, place):
        pltpu.make_async_remote_copy(
            src_ref=src,
            dst_ref=dst,
            send_sem=send_sem.at[send_s],
            recv_sem=recv_sem.at[recv_s],
            device_id=device(*place),
            device_id_type=MESH,
        ).start()

    def wait_bytes(sem, ref):
        pltpu.make_async_copy(ref, ref, sem).wait()

    unfinished = []

    def finish():
        for phase, ref in unfinished:
            wait_bytes(send_sem.at[phase], ref)

    barrier = pltpu.get_barrier_semaphore()
    places = [shifted(dx=dx, dy=dy) for dx, dy in reversed(xy_steps[1:])]
    places += [shifted(dz=dz, dc=dc) for dc, dz in zc_steps[:-1]]
    places += [yl_place(dl, dz) for dl, dz in blk_steps if dl and dz]
    for place in places:
        pl.semaphore_signal(barrier, inc=1, device_id=device(*place), device_id_type=MESH)

    inputs = [
        pltpu.make_async_copy(src, dst, recv_sem.at[INP + i])
        for i, (src, dst) in enumerate(
            (
                (crd_hbm, crd_ref),
                (area_hbm, area_ref),
                (loads_hbm, loads_ref),
                (rec_hbm, rec_ref),
                (shp_hbm, shp_ref),
                (cpl_hbm, cpl_ref),
            )
        )
    ]
    for copy in inputs:
        copy.start()
    inputs[0].wait()
    inputs[1].wait()
    half_scale = 0.5 * WAVE / math.pi
    geo_s[0, 0:3, :] = crd_ref[...] * half_scale
    geo_s[0, 3:4, :] = area_ref[...] * (half_scale * half_scale / total_panels)
    geo_t[n_zc - 1, :, :] = geo_s[0, :, :]
    inputs[2].wait()
    inputs[3].wait()
    loads = loads_ref[...]
    loads_rot = rotated(loads.astype(F32)).astype(BF16)
    psum = jnp.dot(rec_ref[0], loads, preferred_element_type=F32) + jnp.dot(
        rec_ref[1], loads_rot, preferred_element_type=F32
    )
    part[...] = psum.reshape(n_blk, RW, CW)
    part_h[...] = psum.astype(BF16).reshape(n_blk, RW, CW)

    pl.semaphore_wait(barrier, len(places))

    for q, (dl, dz) in enumerate(blk_steps):
        place = yl_place(dl, dz)
        owner = lax.rem(place[1], YL) * Z + place[2]
        send(RS_AMP, RS_AMP, part_h.at[owner], amp_in.at[q], place)
    for n in range(1, n_xy):
        dx, dy = xy_steps[n]
        send(GEO_S, GEO_S, geo_s.at[0], geo_s.at[n], shifted(dx=dx, dy=dy))
    for t in range(n_zc - 1):
        dc, dz = zc_steps[t]
        send(GEO_T, GEO_T, geo_t.at[n_zc - 1], geo_t.at[t], shifted(dz=dz, dc=dc))
    unfinished.append((GEO_S, geo_s.at[pl.ds(1, n_xy - 1)]))
    unfinished.append((GEO_T, geo_t.at[pl.ds(1, n_zc - 1)]))
    unfinished.append((RS_AMP, amp_in))

    def prepare():
        inputs[4].wait()
        area_b[...] = turn_rows(area_ref[...])
        shp_f[...] = shp_ref[...].astype(F32).reshape(PB * KB, mb)
        for k in range(KB):
            block = shp_f[pl.ds(k, PB, stride=KB), :]
            shp_k[k] = block.astype(BF16)
            shp_t[k] = jnp.transpose(block).astype(BF16)
        cbuf[KB] = jnp.zeros((2, X, RW, CW), BF16)
        inputs[5].wait()

        def fill_inv(j, carry):
            found = jnp.int32(KB)
            for k in range(KB):
                found = jnp.where(cpl_ref[0, k] == j, jnp.int32(k), found)
            inv[j] = found
            return carry

        lax.fori_loop(0, n_blk * YH, fill_inv, 0)

    def turn_step(slot, carry):
        rows = pl.ds(pl.multiple_of(slot * PB, PB), PB)
        for axis in range(3):
            tgt_b[axis, rows, :] = turn_rows(geo_t[slot, axis : axis + 1, :])
        return carry

    steps = n_zc * PB // ROWS

    def kernel_chunks(lo, hi):
        def chunk(d, carry):
            shape = (ROWS, PB)
            sx = jnp.broadcast_to(geo_s[d, 0:1, :], shape)
            sy = jnp.broadcast_to(geo_s[d, 1:2, :], shape)
            sz = jnp.broadcast_to(geo_s[d, 2:3, :], shape)
            sa = jnp.broadcast_to(geo_s[d, 3:4, :], shape)

            def rows_step(i, inner):
                rows = pl.ds(pl.multiple_of(i * ROWS, ROWS), ROWS)
                dx = tgt_b[0, rows, :] - sx
                dy = tgt_b[1, rows, :] - sy
                dz = tgt_b[2, rows, :] - sz
                d2 = dx * dx + dy * dy + dz * dz + sa
                r = lax.rsqrt(d2)
                h = d2 * r
                f = h - jnp.round(h)
                u = f * f
                s = horner(SIN, u) * f
                c = horner(COS, u)
                rs = r * s
                kmat[d, rows, 0:PB] = (r - rs * s).astype(BF16)
                kmat[d, rows, PB : 2 * PB] = (rs * c).astype(BF16)
                return inner

            return lax.fori_loop(0, steps, rows_step, carry)

        lax.fori_loop(lo, hi, chunk, 0)

    cuts = [round(n_xy * part_of / 16) for part_of in CUTS]

    prepare()

    wait_bytes(recv_sem.at[RS_AMP], amp_in)
    asum = part[blk]
    for q in range(n_blk - 1):
        asum = asum + amp_in[q].astype(F32)
    xl = x * YL + yl
    amp[core, yh, xl, z] = asum.astype(BF16)
    for dz in z_steps[:-1]:
        mine = amp.at[core, yh, xl, z]
        send(AG_Z, AG_Z, mine, mine, shifted(dz=dz))
    seven = amp.at[0, 0, 0, pl.ds(0, Z - 1)]
    unfinished.append((AG_Z, seven))

    wait_bytes(recv_sem.at[GEO_T], geo_t.at[pl.ds(1, n_zc - 1)])
    lax.fori_loop(0, n_zc, turn_step, 0)
    wait_bytes(recv_sem.at[GEO_S], geo_s.at[pl.ds(1, n_xy - 1)])
    kernel_chunks(0, cuts[0])
    wait_bytes(recv_sem.at[AG_Z], seven)
    mine = amp.at[core, yh, xl]

    def send_block(g):
        for n in groups[g]:
            dx, dy = xy_steps[n]
            if n:
                send(AG_XY, AG_XY + g, mine, mine, shifted(dx=dx, dy=dy))

    send_block(2)
    send_block(1)
    kernel_chunks(cuts[0], cuts[1])
    send_block(0)
    unfinished.append((AG_XY, vels.at[pl.ds(1, n_xy - 1), pl.ds(0, mb)]))
    kernel_chunks(cuts[1], cuts[4])
    for g in (2, 1, 0):
        rest = [n for n in groups[g] if n]
        if rest:
            wait_bytes(recv_sem.at[AG_XY + g], vels.at[pl.ds(1, len(rest)), pl.ds(0, mb)])
    half_amp = amp.at[core]
    send(AG_C, AG_C, half_amp, half_amp, shifted(dc=1))
    unfinished.append((AG_C, half_amp))
    kernel_chunks(cuts[4], cuts[5])
    wait_bytes(recv_sem.at[AG_C], half_amp)

    vel = jnp.zeros((PB, CW), F32)
    for k in range(KB):
        j = cpl_ref[0, k]
        jl = lax.rem(j, X * YL)
        jc = lax.rem(lax.div(j, X * YL), 2)
        jh = lax.div(j, X * YL * 2)
        block = amp[jc, jh, jl].reshape(mb, CW)
        vel = vel + jnp.dot(shp_k[k], block, preferred_element_type=F32)
    vels[0] = (vel * area_b[...] * (half_scale / math.sqrt(total_panels))).astype(BF16)
    for g, group in enumerate(groups):
        for n in group:
            dx, dy = xy_steps[n]
            if n:
                batch = [n in b for b in batches].index(True)
                send(VEL, VEL + batch, vels.at[0], vels.at[n], shifted(dx=dx, dy=dy))
    kernel_chunks(cuts[5], n_xy)
    unfinished.append((VEL, vels.at[pl.ds(1, n_xy - 1)]))

    def weights(g):
        group = batches[g]
        rest = [n for n in group if n]
        if rest:
            wait_bytes(recv_sem.at[VEL + g], vels.at[pl.ds(rest[0], len(rest))])
        for n in group:
            value = vels[n]
            w_ref[n, 0:PB, :] = value
            w_ref[n, PB : 2 * PB, :] = rotated(value.astype(F32)).astype(BF16)

    def products(g, rows):
        total = None
        for n in batches[g]:
            term = jnp.dot(kmat[n, rows, :], w_ref[n], preferred_element_type=F32)
            total = term if total is None else total + term
        return total

    mm_rows = min(1024, n_zc * PB)
    last = len(batches) - 1
    for g in range(last):
        weights(g)

        def mm_step(i, carry):
            rows = pl.ds(pl.multiple_of(i * mm_rows, mm_rows), mm_rows)
            prod = products(g, rows)
            acc[rows, :] = prod if g == 0 else acc[rows, :] + prod
            return carry

        lax.fori_loop(0, n_zc * PB // mm_rows, mm_step, 0)

    weights(last)
    pair = 2
    n_pair = Z // pair

    def other_core(i):
        rows = pl.ds(pl.multiple_of(i * (pair * PB), pair * PB), pair * PB)
        value = acc[rows, :] + products(last, rows)
        p_out[i] = value.astype(BF16).reshape(pair, PB, CW)
        send(RS_PC, RS_PC + i, p_out.at[i], pc_in.at[i], shifted(dc=1))

    def this_core(i, final=False):
        rows = pl.ds(pl.multiple_of((n_pair + i) * (pair * PB), pair * PB), pair * PB)
        value = acc[rows, :] + products(last, rows)
        wait_bytes(recv_sem.at[RS_PC + i], pc_in.at[i])
        value = value + pc_in[i].astype(F32).reshape(pair * PB, CW)
        for h in range(pair):
            t = i * pair + h
            part_p = value[h * PB : (h + 1) * PB]
            if final and h == pair - 1:
                return part_p
            back = Z // 2 + i + 1 if h else Z // 2 - i
            pz_out[t] = part_p.astype(BF16)
            send(RS_PZ, RS_PZ, pz_out.at[t], pz_in.at[t], shifted(dz=back))

    def first_steps(i, carry):
        other_core(i)
        return carry

    def middle_steps(i, carry):
        other_core(i + ahead)
        this_core(i)
        return carry

    def later_steps(i, carry):
        this_core(i)
        return carry

    ahead = min(2, n_pair)
    lax.fori_loop(0, ahead, first_steps, 0)
    lax.fori_loop(0, n_pair - ahead, middle_steps, 0)
    lax.fori_loop(n_pair - ahead, n_pair - 1, later_steps, 0)
    total = this_core(n_pair - 1, final=True)
    unfinished.append((RS_PC, p_out))
    unfinished.append((RS_PZ, pz_in))
    wait_bytes(recv_sem.at[RS_PZ], pz_in)
    for t in range(Z - 1):
        total = total + pz_in[t].astype(F32)
    pressure = total.astype(BF16)
    prs_ref[...] = pressure
    weighted = (area_b[...] * pressure.astype(F32)).astype(BF16)

    for k in range(KB):
        cbuf[k] = (
            jnp.dot(shp_t[k], weighted, preferred_element_type=F32)
            .astype(BF16)
            .reshape(2, X, RW, CW)
        )
    other = 1 - core
    for n, dy in enumerate(y_steps):
        y_ = lax.rem(y + dy, Y)
        first = lax.rem(y_, YL) * (Z * YH) + lax.div(y_, YL)
        for zz in range(Z):
            lc_out[n, zz] = cbuf[inv[first + zz * YH], other]
        send(RS_LC, RS_LC + n, lc_out.at[n], lc_in.at[n], shifted(dc=1))
    unfinished.append((RS_LC, lc_out))
    lx_slot = 0
    for n, dy in enumerate(y_steps):
        y_ = lax.rem(y + dy, Y)
        first = lax.rem(y_, YL) * (Z * YH) + lax.div(y_, YL)
        wait_bytes(recv_sem.at[RS_LC + n], lc_in.at[n])
        for zz in range(Z):
            both = cbuf[inv[first + zz * YH], core].astype(F32) + lc_in[n, zz].astype(F32)
            for xx in range(X):
                lx_out[n, xx, zz] = both[xx].astype(BF16)
                if dy == 0:
                    lx_own[xx, zz] = both[xx]
        for dx in sorted(range(X), key=lambda q: -near(q, X)):
            if dx or dy:
                place = shifted(dx=dx, dy=dy)
                send(RS_LXY, RS_LXY, lx_out.at[n, place[0]], lx_in.at[lx_slot], place)
                lx_slot += 1
    unfinished.append((RS_LXY, lx_in))
    wait_bytes(recv_sem.at[RS_LXY], lx_in)
    lsum = lx_own[x]
    for q in range(n_xy - 1):
        lsum = lsum + lx_in[q].astype(F32)
    lx_own[x] = lsum
    lz_out[...] = lsum.astype(BF16)
    for t, dz in enumerate(z_steps[:-1]):
        place = shifted(dz=dz)
        send(RS_LZ, RS_LZ, lz_out.at[place[2]], lz_in.at[t], place)
    unfinished.append((RS_LZ, lz_in))
    fin = lx_own[x, z]
    wait_bytes(recv_sem.at[RS_LZ], lz_in)
    for t in range(Z - 1):
        fin = fin + lz_in[t].astype(F32)
    out_ref[...] = fin
    finish()


def copy_kernel(a_ref, b_ref, c_ref, d_ref):
    c_ref[...] = a_ref[...]
    d_ref[...] = b_ref[...]


def solution(mesh):
    Z = mesh.shape["blk"] // YL
    YH = mesh.shape["tgt"] // 2
    X = mesh.shape["sec"]
    Y = YH * YL
    n_xy, n_zc, n_blk = X * Y, 2 * Z, YL * Z
    mb = Z * RW

    def on_device(modal_loads, receptance, shapes, coupling, panel_coords, panel_areas):
        KB = shapes.shape[1]
        scratch = [
            pltpu.VMEM(modal_loads.shape, BF16),
            pltpu.VMEM(receptance.shape, BF16),
            pltpu.VMEM(shapes.shape, BF16),
            pltpu.SMEM(coupling.shape, jnp.int32),
            pltpu.VMEM(panel_coords.shape, F32),
            pltpu.VMEM((1, PB), F32),
            pltpu.VMEM((n_xy, 4, PB), F32),
            pltpu.VMEM((n_zc, 4, PB), F32),
            pltpu.VMEM((3, n_zc * PB, PB), F32),
            pltpu.VMEM((PB, PB), F32),
            pltpu.VMEM((n_xy, n_zc * PB, 2 * PB), BF16),
            pltpu.VMEM((n_zc * PB, CW), F32),
            pltpu.VMEM((n_blk, RW, CW), F32),
            pltpu.VMEM((n_blk, RW, CW), BF16),
            pltpu.VMEM((n_blk - 1, RW, CW), BF16),
            pltpu.VMEM((2, YH, X * YL, Z, RW, CW), BF16),
            pltpu.VMEM((n_xy, PB, CW), BF16),
            pltpu.VMEM((n_xy, 2 * PB, CW), BF16),
            pltpu.VMEM((Z // 2, 2, PB, CW), BF16),
            pltpu.VMEM((Z // 2, 2, PB, CW), BF16),
            pltpu.VMEM((Z - 1, PB, CW), BF16),
            pltpu.VMEM((Z - 1, PB, CW), BF16),
            pltpu.VMEM((PB * KB, mb), F32),
            pltpu.VMEM((KB, PB, mb), BF16),
            pltpu.VMEM((KB, mb, PB), BF16),
            pltpu.SMEM((n_blk * YH,), jnp.int32),
            pltpu.VMEM((KB + 1, 2, X, RW, CW), BF16),
            pltpu.VMEM((Y, Z, X, RW, CW), BF16),
            pltpu.VMEM((Y, Z, X, RW, CW), BF16),
            pltpu.VMEM((Y, X, Z, RW, CW), BF16),
            pltpu.VMEM((n_xy - 1, Z, RW, CW), BF16),
            pltpu.VMEM((X, Z, RW, CW), F32),
            pltpu.VMEM((Z, RW, CW), BF16),
            pltpu.VMEM((Z - 1, RW, CW), BF16),
            pltpu.SemaphoreType.DMA((N_SEM,)),
            pltpu.SemaphoreType.DMA((N_SEM,)),
        ]
        vmem = pl.BlockSpec(memory_space=pltpu.VMEM)
        outs = (
            jax.ShapeDtypeStruct((RW, CW), F32),
            jax.ShapeDtypeStruct((PB, CW), BF16),
        )
        results = pl.pallas_call(
            functools.partial(kernel, (X, YH, Z, KB)),
            out_shape=outs,
            in_specs=[pl.BlockSpec(memory_space=pl.ANY)] * 6,
            out_specs=(vmem, vmem),
            scratch_shapes=scratch,
            compiler_params=pltpu.CompilerParams(
                collective_id=0,
                has_side_effects=True,
                vmem_limit_bytes=58 * 1024 * 1024,
            ),
        )(
            modal_loads,
            receptance,
            shapes,
            coupling,
            panel_coords,
            panel_areas.reshape(1, PB),
        )
        return pl.pallas_call(
            copy_kernel,
            out_shape=outs,
            in_specs=[vmem, vmem],
            out_specs=(vmem, vmem),
        )(*results)

    owned = ("blk", "tgt", "sec")
    in_specs = (
        P("blk", None),
        P(None, ("tgt", "sec"), "blk"),
        P(owned, None, None),
        P(owned, None),
        P(None, owned),
        P(owned),
    )
    return jax.shard_map(
        on_device,
        mesh=mesh,
        in_specs=in_specs,
        out_specs=(P(owned, None), P(owned, None)),
        check_vma=False,
    )
```

```python
import functools
import math

import jax
import jax.numpy as jnp
from jax import lax
from jax.experimental import pallas as pl
from jax.experimental.pallas import tpu as pltpu
from jax.sharding import PartitionSpec as P

MESH = pl.DeviceIdType.MESH
F32 = jnp.float32
BF16 = jnp.bfloat16

WAVE = 40.0
YL = 2
PB = 128
CW = 128
RW = 16
ROWS = 256

CUTS = (2, 4, 7, 9, 10, 11)

SIN = (4.442879567546083, -7.307816684491776, 3.5977741780871795, -0.7911993921612632)
COS = (1.4142040148090755, -6.977637323456285, 5.715187874756681, -1.7282138922234693)

GEO_S, GEO_T, RS_AMP, AG_Z, AG_C, RS_PZ, RS_LXY, RS_LZ, AG_XY, VEL, RS_PC, RS_LC, INP, N_SEM = (
    0, 1, 2, 3, 4, 5, 6, 7, 8, 12, 16, 20, 24, 30,
)


def horner(coefs, u):
    acc = u * coefs[-1] + coefs[-2]
    for value in coefs[-3::-1]:
        acc = acc * u + value
    return acc


def turn_rows(value):
    n = value.shape[1]
    return jnp.transpose(jnp.broadcast_to(value, (n, n)))


def rotated(value):
    half = value.shape[1] // 2
    turned = pltpu.roll(value, half, 1)
    lane = lax.broadcasted_iota(jnp.int32, value.shape, 1)
    return jnp.where(lane < half, -turned, turned)


def near(d, n):
    return min(d, n - d)


def kernel(
    dims,
    loads_hbm,
    rec_hbm,
    shp_hbm,
    cpl_hbm,
    crd_hbm,
    area_hbm,
    out_ref,
    prs_ref,
    loads_ref,
    rec_ref,
    shp_ref,
    cpl_ref,
    crd_ref,
    area_ref,
    geo_s,
    geo_t,
    tgt_b,
    area_b,
    kmat,
    acc,
    part,
    part_h,
    amp_in,
    amp,
    vels,
    w_ref,
    p_out,
    pc_in,
    pz_out,
    pz_in,
    shp_f,
    shp_k,
    shp_t,
    inv,
    cbuf,
    lc_out,
    lc_in,
    lx_out,
    lx_in,
    lx_own,
    lz_out,
    lz_in,
    send_sem,
    recv_sem,
):
    X, YH, Z, KB = dims
    Y = YH * YL
    n_xy, n_zc, n_blk = X * Y, 2 * Z, YL * Z
    mb = Z * RW
    total_panels = float(PB * 2 * X * Y * Z)

    blk, tgt, sec = lax.axis_index("blk"), lax.axis_index("tgt"), lax.axis_index("sec")
    yl, z = lax.div(blk, Z), lax.rem(blk, Z)
    yh, core = lax.div(tgt, 2), lax.rem(tgt, 2)
    x = sec
    y = yh * YL + yl

    def device(x_, y_, z_, c_):
        return (lax.rem(y_, YL) * Z + z_, lax.div(y_, YL) * 2 + c_, x_)

    def shifted(dx=0, dy=0, dz=0, dc=0):
        return (
            lax.rem(x + dx, X),
            lax.rem(y + dy, Y),
            lax.rem(z + dz, Z),
            lax.rem(core + dc, 2),
        )

    xy_steps = sorted(((q % X, q // X) for q in range(n_xy)), key=lambda s: near(s[0], X) + near(s[1], Y))
    z_steps = sorted(range(Z), key=lambda q: -near(q, Z))
    zc_steps = [(dc, dz) for dc in (1, 0) for dz in z_steps]
    y_steps = sorted(range(Y), key=lambda q: -near(q, Y))
    blk_steps = sorted(
        ((dl, dz) for dl in range(YL) for dz in range(Z) if dl or dz), key=lambda s: -s[0] - near(s[1], Z)
    )
    edges = (0, min(5, n_xy - 2), min(11, n_xy - 1), n_xy)
    used = (0, min(5, n_xy - 2), min(11, n_xy - 1), n_xy)
    groups = [range(lo, hi) for lo, hi in zip(edges, edges[1:])]
    batches = [range(lo, hi) for lo, hi in zip(used, used[1:])]

    def yl_place(dl, dz):
        y_ = yh * YL + lax.rem(yl + dl, YL)
        return (x, y_, lax.rem(z + dz, Z), core)

    def send(send_s, recv_s, src, dst, place):
        pltpu.make_async_remote_copy(
            src_ref=src,
            dst_ref=dst,
            send_sem=send_sem.at[send_s],
            recv_sem=recv_sem.at[recv_s],
            device_id=device(*place),
            device_id_type=MESH,
        ).start()

    def wait_bytes(sem, ref):
        pltpu.make_async_copy(ref, ref, sem).wait()

    unfinished = []

    def finish():
        for phase, ref in unfinished:
            wait_bytes(send_sem.at[phase], ref)

    barrier = pltpu.get_barrier_semaphore()
    places = [shifted(dx=dx, dy=dy) for dx, dy in reversed(xy_steps[1:])]
    places += [shifted(dz=dz, dc=dc) for dc, dz in zc_steps[:-1]]
    places += [yl_place(dl, dz) for dl, dz in blk_steps if dl and dz]
    for place in places:
        pl.semaphore_signal(barrier, inc=1, device_id=device(*place), device_id_type=MESH)

    inputs = [
        pltpu.make_async_copy(src, dst, recv_sem.at[INP + i])
        for i, (src, dst) in enumerate(
            (
                (crd_hbm, crd_ref),
                (area_hbm, area_ref),
                (loads_hbm, loads_ref),
                (rec_hbm, rec_ref),
                (shp_hbm, shp_ref),
                (cpl_hbm, cpl_ref),
            )
        )
    ]
    for copy in inputs:
        copy.start()
    inputs[0].wait()
    inputs[1].wait()
    half_scale = 0.5 * WAVE / math.pi
    geo_s[0, 0:3, :] = crd_ref[...] * half_scale
    geo_s[0, 3:4, :] = area_ref[...] * (half_scale * half_scale / total_panels)
    geo_t[n_zc - 1, :, :] = geo_s[0, :, :]
    inputs[2].wait()
    inputs[3].wait()
    loads = loads_ref[...]
    loads_rot = rotated(loads.astype(F32)).astype(BF16)
    psum = jnp.dot(rec_ref[0], loads, preferred_element_type=F32) + jnp.dot(
        rec_ref[1], loads_rot, preferred_element_type=F32
    )
    part[...] = psum.reshape(n_blk, RW, CW)
    part_h[...] = psum.astype(BF16).reshape(n_blk, RW, CW)

    pl.semaphore_wait(barrier, len(places))

    for q, (dl, dz) in enumerate(blk_steps):
        place = yl_place(dl, dz)
        owner = lax.rem(place[1], YL) * Z + place[2]
        send(RS_AMP, RS_AMP, part_h.at[owner], amp_in.at[q], place)
    for n in range(1, n_xy):
        dx, dy = xy_steps[n]
        send(GEO_S, GEO_S, geo_s.at[0], geo_s.at[n], shifted(dx=dx, dy=dy))
    for t in range(n_zc - 1):
        dc, dz = zc_steps[t]
        send(GEO_T, GEO_T, geo_t.at[n_zc - 1], geo_t.at[t], shifted(dz=dz, dc=dc))
    unfinished.append((GEO_S, geo_s.at[pl.ds(1, n_xy - 1)]))
    unfinished.append((GEO_T, geo_t.at[pl.ds(1, n_zc - 1)]))
    unfinished.append((RS_AMP, amp_in))

    def prepare():
        inputs[4].wait()
        area_b[...] = turn_rows(area_ref[...])
        shp_f[...] = shp_ref[...].astype(F32).reshape(PB * KB, mb)
        for k in range(KB):
            block = shp_f[pl.ds(k, PB, stride=KB), :]
            shp_k[k] = block.astype(BF16)
            shp_t[k] = jnp.transpose(block).astype(BF16)
        cbuf[KB] = jnp.zeros((2, X, RW, CW), BF16)
        inputs[5].wait()

        def fill_inv(j, carry):
            found = jnp.int32(KB)
            for k in range(KB):
                found = jnp.where(cpl_ref[0, k] == j, jnp.int32(k), found)
            inv[j] = found
            return carry

        lax.fori_loop(0, n_blk * YH, fill_inv, 0)

    def turn_step(slot, carry):
        rows = pl.ds(pl.multiple_of(slot * PB, PB), PB)
        for axis in range(3):
            tgt_b[axis, rows, :] = turn_rows(geo_t[slot, axis : axis + 1, :])
        return carry

    steps = n_zc * PB // ROWS

    def kernel_chunks(lo, hi):
        def chunk(d, carry):
            shape = (ROWS, PB)
            sx = jnp.broadcast_to(geo_s[d, 0:1, :], shape)
            sy = jnp.broadcast_to(geo_s[d, 1:2, :], shape)
            sz = jnp.broadcast_to(geo_s[d, 2:3, :], shape)
            sa = jnp.broadcast_to(geo_s[d, 3:4, :], shape)

            def rows_step(i, inner):
                rows = pl.ds(pl.multiple_of(i * ROWS, ROWS), ROWS)
                dx = tgt_b[0, rows, :] - sx
                dy = tgt_b[1, rows, :] - sy
                dz = tgt_b[2, rows, :] - sz
                d2 = dx * dx + dy * dy + dz * dz + sa
                r = lax.rsqrt(d2)
                h = d2 * r
                f = h - jnp.round(h)
                u = f * f
                s = horner(SIN, u) * f
                c = horner(COS, u)
                rs = r * s
                kmat[d, rows, 0:PB] = (r - rs * s).astype(BF16)
                kmat[d, rows, PB : 2 * PB] = (rs * c).astype(BF16)
                return inner

            return lax.fori_loop(0, steps, rows_step, carry)

        lax.fori_loop(lo, hi, chunk, 0)

    cuts = [round(n_xy * part_of / 16) for part_of in CUTS]

    prepare()

    wait_bytes(recv_sem.at[RS_AMP], amp_in)
    asum = part[blk]
    for q in range(n_blk - 1):
        asum = asum + amp_in[q].astype(F32)
    xl = x * YL + yl
    amp[core, yh, xl, z] = asum.astype(BF16)
    for dz in z_steps[:-1]:
        mine = amp.at[core, yh, xl, z]
        send(AG_Z, AG_Z, mine, mine, shifted(dz=dz))
    seven = amp.at[0, 0, 0, pl.ds(0, Z - 1)]
    unfinished.append((AG_Z, seven))

    wait_bytes(recv_sem.at[GEO_T], geo_t.at[pl.ds(1, n_zc - 1)])
    lax.fori_loop(0, n_zc, turn_step, 0)
    wait_bytes(recv_sem.at[GEO_S], geo_s.at[pl.ds(1, n_xy - 1)])
    kernel_chunks(0, cuts[0])
    wait_bytes(recv_sem.at[AG_Z], seven)
    mine = amp.at[core, yh, xl]

    def send_block(g):
        for n in groups[g]:
            dx, dy = xy_steps[n]
            if n:
                send(AG_XY, AG_XY + g, mine, mine, shifted(dx=dx, dy=dy))

    send_block(2)
    send_block(1)
    kernel_chunks(cuts[0], cuts[1])
    send_block(0)
    unfinished.append((AG_XY, vels.at[pl.ds(1, n_xy - 1), pl.ds(0, mb)]))
    kernel_chunks(cuts[1], cuts[4])
    for g in (2, 1, 0):
        rest = [n for n in groups[g] if n]
        if rest:
            wait_bytes(recv_sem.at[AG_XY + g], vels.at[pl.ds(1, len(rest)), pl.ds(0, mb)])
    half_amp = amp.at[core]
    send(AG_C, AG_C, half_amp, half_amp, shifted(dc=1))
    unfinished.append((AG_C, half_amp))
    kernel_chunks(cuts[4], cuts[5])
    wait_bytes(recv_sem.at[AG_C], half_amp)

    vel = jnp.zeros((PB, CW), F32)
    for k in range(KB):
        j = cpl_ref[0, k]
        jl = lax.rem(j, X * YL)
        jc = lax.rem(lax.div(j, X * YL), 2)
        jh = lax.div(j, X * YL * 2)
        block = amp[jc, jh, jl].reshape(mb, CW)
        vel = vel + jnp.dot(shp_k[k], block, preferred_element_type=F32)
    vels[0] = (vel * area_b[...] * (half_scale / math.sqrt(total_panels))).astype(BF16)
    for g, group in enumerate(groups):
        for n in group:
            dx, dy = xy_steps[n]
            if n:
                batch = [n in b for b in batches].index(True)
                send(VEL, VEL + batch, vels.at[0], vels.at[n], shifted(dx=dx, dy=dy))
    kernel_chunks(cuts[5], n_xy)
    unfinished.append((VEL, vels.at[pl.ds(1, n_xy - 1)]))

    def weights(g):
        group = batches[g]
        rest = [n for n in group if n]
        if rest:
            wait_bytes(recv_sem.at[VEL + g], vels.at[pl.ds(rest[0], len(rest))])
        for n in group:
            value = vels[n]
            w_ref[n, 0:PB, :] = value
            w_ref[n, PB : 2 * PB, :] = rotated(value.astype(F32)).astype(BF16)

    def products(g, rows):
        total = None
        for n in batches[g]:
            term = jnp.dot(kmat[n, rows, :], w_ref[n], preferred_element_type=F32)
            total = term if total is None else total + term
        return total

    mm_rows = min(1024, n_zc * PB)
    last = len(batches) - 1
    for g in range(last):
        weights(g)

        def mm_step(i, carry):
            rows = pl.ds(pl.multiple_of(i * mm_rows, mm_rows), mm_rows)
            prod = products(g, rows)
            acc[rows, :] = prod if g == 0 else acc[rows, :] + prod
            return carry

        lax.fori_loop(0, n_zc * PB // mm_rows, mm_step, 0)

    weights(last)
    pair = 2
    n_pair = Z // pair

    def other_core(i):
        rows = pl.ds(pl.multiple_of(i * (pair * PB), pair * PB), pair * PB)
        value = acc[rows, :] + products(last, rows)
        p_out[i] = value.astype(BF16).reshape(pair, PB, CW)
        send(RS_PC, RS_PC + i, p_out.at[i], pc_in.at[i], shifted(dc=1))

    def this_core(i, final=False):
        rows = pl.ds(pl.multiple_of((n_pair + i) * (pair * PB), pair * PB), pair * PB)
        value = acc[rows, :] + products(last, rows)
        wait_bytes(recv_sem.at[RS_PC + i], pc_in.at[i])
        value = value + pc_in[i].astype(F32).reshape(pair * PB, CW)
        for h in range(pair):
            t = i * pair + h
            part_p = value[h * PB : (h + 1) * PB]
            if final and h == pair - 1:
                return part_p
            back = Z // 2 + i + 1 if h else Z // 2 - i
            pz_out[t] = part_p.astype(BF16)
            send(RS_PZ, RS_PZ, pz_out.at[t], pz_in.at[t], shifted(dz=back))

    def first_steps(i, carry):
        other_core(i)
        return carry

    def middle_steps(i, carry):
        other_core(i + ahead)
        this_core(i)
        return carry

    def later_steps(i, carry):
        this_core(i)
        return carry

    ahead = min(2, n_pair)
    lax.fori_loop(0, ahead, first_steps, 0)
    lax.fori_loop(0, n_pair - ahead, middle_steps, 0)
    lax.fori_loop(n_pair - ahead, n_pair - 1, later_steps, 0)
    total = this_core(n_pair - 1, final=True)
    unfinished.append((RS_PC, p_out))
    unfinished.append((RS_PZ, pz_in))
    wait_bytes(recv_sem.at[RS_PZ], pz_in)
    for t in range(Z - 1):
        total = total + pz_in[t].astype(F32)
    pressure = total.astype(BF16)
    prs_ref[...] = pressure
    weighted = (area_b[...] * pressure.astype(F32)).astype(BF16)

    for k in range(KB):
        cbuf[k] = (
            jnp.dot(shp_t[k], weighted, preferred_element_type=F32)
            .astype(BF16)
            .reshape(2, X, RW, CW)
        )
    other = 1 - core
    for n, dy in enumerate(y_steps):
        y_ = lax.rem(y + dy, Y)
        first = lax.rem(y_, YL) * (Z * YH) + lax.div(y_, YL)
        for zz in range(Z):
            lc_out[n, zz] = cbuf[inv[first + zz * YH], other]
        send(RS_LC, RS_LC + n, lc_out.at[n], lc_in.at[n], shifted(dc=1))
    unfinished.append((RS_LC, lc_out))
    lx_slot = 0
    for n, dy in enumerate(y_steps):
        y_ = lax.rem(y + dy, Y)
        first = lax.rem(y_, YL) * (Z * YH) + lax.div(y_, YL)
        wait_bytes(recv_sem.at[RS_LC + n], lc_in.at[n])
        for zz in range(Z):
            both = cbuf[inv[first + zz * YH], core].astype(F32) + lc_in[n, zz].astype(F32)
            for xx in range(X):
                lx_out[n, xx, zz] = both[xx].astype(BF16)
                if dy == 0:
                    lx_own[xx, zz] = both[xx]
        for dx in sorted(range(X), key=lambda q: -near(q, X)):
            if dx or dy:
                place = shifted(dx=dx, dy=dy)
                send(RS_LXY, RS_LXY, lx_out.at[n, place[0]], lx_in.at[lx_slot], place)
                lx_slot += 1
    unfinished.append((RS_LXY, lx_in))
    wait_bytes(recv_sem.at[RS_LXY], lx_in)
    lsum = lx_own[x]
    for q in range(n_xy - 1):
        lsum = lsum + lx_in[q].astype(F32)
    lx_own[x] = lsum
    lz_out[...] = lsum.astype(BF16)
    for t, dz in enumerate(z_steps[:-1]):
        place = shifted(dz=dz)
        send(RS_LZ, RS_LZ, lz_out.at[place[2]], lz_in.at[t], place)
    unfinished.append((RS_LZ, lz_in))
    fin = lx_own[x, z]
    wait_bytes(recv_sem.at[RS_LZ], lz_in)
    for t in range(Z - 1):
        fin = fin + lz_in[t].astype(F32)
    out_ref[...] = fin
    finish()


def copy_kernel(a_ref, b_ref, c_ref, d_ref):
    c_ref[...] = a_ref[...]
    d_ref[...] = b_ref[...]


def solution(mesh):
    Z = mesh.shape["blk"] // YL
    YH = mesh.shape["tgt"] // 2
    X = mesh.shape["sec"]
    Y = YH * YL
    n_xy, n_zc, n_blk = X * Y, 2 * Z, YL * Z
    mb = Z * RW

    def on_device(modal_loads, receptance, shapes, coupling, panel_coords, panel_areas):
        KB = shapes.shape[1]
        scratch = [
            pltpu.VMEM(modal_loads.shape, BF16),
            pltpu.VMEM(receptance.shape, BF16),
            pltpu.VMEM(shapes.shape, BF16),
            pltpu.SMEM(coupling.shape, jnp.int32),
            pltpu.VMEM(panel_coords.shape, F32),
            pltpu.VMEM((1, PB), F32),
            pltpu.VMEM((n_xy, 4, PB), F32),
            pltpu.VMEM((n_zc, 4, PB), F32),
            pltpu.VMEM((3, n_zc * PB, PB), F32),
            pltpu.VMEM((PB, PB), F32),
            pltpu.VMEM((n_xy, n_zc * PB, 2 * PB), BF16),
            pltpu.VMEM((n_zc * PB, CW), F32),
            pltpu.VMEM((n_blk, RW, CW), F32),
            pltpu.VMEM((n_blk, RW, CW), BF16),
            pltpu.VMEM((n_blk - 1, RW, CW), BF16),
            pltpu.VMEM((2, YH, X * YL, Z, RW, CW), BF16),
            pltpu.VMEM((n_xy, PB, CW), BF16),
            pltpu.VMEM((n_xy, 2 * PB, CW), BF16),
            pltpu.VMEM((Z // 2, 2, PB, CW), BF16),
            pltpu.VMEM((Z // 2, 2, PB, CW), BF16),
            pltpu.VMEM((Z - 1, PB, CW), BF16),
            pltpu.VMEM((Z - 1, PB, CW), BF16),
            pltpu.VMEM((PB * KB, mb), F32),
            pltpu.VMEM((KB, PB, mb), BF16),
            pltpu.VMEM((KB, mb, PB), BF16),
            pltpu.SMEM((n_blk * YH,), jnp.int32),
            pltpu.VMEM((KB + 1, 2, X, RW, CW), BF16),
            pltpu.VMEM((Y, Z, X, RW, CW), BF16),
            pltpu.VMEM((Y, Z, X, RW, CW), BF16),
            pltpu.VMEM((Y, X, Z, RW, CW), BF16),
            pltpu.VMEM((n_xy - 1, Z, RW, CW), BF16),
            pltpu.VMEM((X, Z, RW, CW), F32),
            pltpu.VMEM((Z, RW, CW), BF16),
            pltpu.VMEM((Z - 1, RW, CW), BF16),
            pltpu.SemaphoreType.DMA((N_SEM,)),
            pltpu.SemaphoreType.DMA((N_SEM,)),
        ]
        vmem = pl.BlockSpec(memory_space=pltpu.VMEM)
        outs = (
            jax.ShapeDtypeStruct((RW, CW), F32),
            jax.ShapeDtypeStruct((PB, CW), BF16),
        )
        results = pl.pallas_call(
            functools.partial(kernel, (X, YH, Z, KB)),
            out_shape=outs,
            in_specs=[pl.BlockSpec(memory_space=pl.ANY)] * 6,
            out_specs=(vmem, vmem),
            scratch_shapes=scratch,
            compiler_params=pltpu.CompilerParams(
                collective_id=0,
                has_side_effects=True,
                vmem_limit_bytes=58 * 1024 * 1024,
            ),
        )(
            modal_loads,
            receptance,
            shapes,
            coupling,
            panel_coords,
            panel_areas.reshape(1, PB),
        )
        return pl.pallas_call(
            copy_kernel,
            out_shape=outs,
            in_specs=[vmem, vmem],
            out_specs=(vmem, vmem),
        )(*results)

    owned = ("blk", "tgt", "sec")
    in_specs = (
        P("blk", None),
        P(None, ("tgt", "sec"), "blk"),
        P(owned, None, None),
        P(owned, None),
        P(None, owned),
        P(owned),
    )
    return jax.shard_map(
        on_device,
        mesh=mesh,
        in_specs=in_specs,
        out_specs=(P(owned, None), P(owned, None)),
        check_vma=False,
    )
```

```python
import functools
import math

import jax
import jax.numpy as jnp
from jax import lax
from jax.experimental import pallas as pl
from jax.experimental.pallas import tpu as pltpu
from jax.sharding import PartitionSpec as P

MESH = pl.DeviceIdType.MESH
F32 = jnp.float32
BF16 = jnp.bfloat16

WAVE = 40.0
YL = 2
PB = 128
CW = 128
RW = 16
ROWS = 256

CUTS = (2, 4, 7, 9, 10, 11)

SIN = (4.442879567546083, -7.307816684491776, 3.5977741780871795, -0.7911993921612632)
COS = (1.4142040148090755, -6.977637323456285, 5.715187874756681, -1.7282138922234693)

GEO_S, GEO_T, RS_AMP, AG_Z, AG_C, RS_PZ, RS_LXY, RS_LZ, AG_XY, VEL, RS_PC, RS_LC, INP, N_SEM = (
    0, 1, 2, 3, 4, 5, 6, 7, 8, 12, 16, 20, 24, 30,
)


def horner(coefs, u):
    acc = u * coefs[-1] + coefs[-2]
    for value in coefs[-3::-1]:
        acc = acc * u + value
    return acc


def turn_rows(value):
    n = value.shape[1]
    return jnp.transpose(jnp.broadcast_to(value, (n, n)))


def rotated(value):
    half = value.shape[1] // 2
    turned = pltpu.roll(value, half, 1)
    lane = lax.broadcasted_iota(jnp.int32, value.shape, 1)
    return jnp.where(lane < half, -turned, turned)


def near(d, n):
    return min(d, n - d)


def kernel(
    dims,
    loads_hbm,
    rec_hbm,
    shp_hbm,
    cpl_hbm,
    crd_hbm,
    area_hbm,
    out_ref,
    prs_ref,
    loads_ref,
    rec_ref,
    shp_ref,
    cpl_ref,
    crd_ref,
    area_ref,
    geo_s,
    geo_t,
    tgt_b,
    area_b,
    kmat,
    acc,
    part,
    part_h,
    amp_in,
    amp,
    vels,
    w_ref,
    p_out,
    pc_in,
    pz_out,
    pz_in,
    shp_f,
    shp_k,
    shp_t,
    inv,
    cbuf,
    lc_out,
    lc_in,
    lx_out,
    lx_in,
    lx_own,
    lz_out,
    lz_in,
    send_sem,
    recv_sem,
):
    X, YH, Z, KB = dims
    Y = YH * YL
    n_xy, n_zc, n_blk = X * Y, 2 * Z, YL * Z
    mb = Z * RW
    total_panels = float(PB * 2 * X * Y * Z)

    blk, tgt, sec = lax.axis_index("blk"), lax.axis_index("tgt"), lax.axis_index("sec")
    yl, z = lax.div(blk, Z), lax.rem(blk, Z)
    yh, core = lax.div(tgt, 2), lax.rem(tgt, 2)
    x = sec
    y = yh * YL + yl

    def device(x_, y_, z_, c_):
        return (lax.rem(y_, YL) * Z + z_, lax.div(y_, YL) * 2 + c_, x_)

    def shifted(dx=0, dy=0, dz=0, dc=0):
        return (
            lax.rem(x + dx, X),
            lax.rem(y + dy, Y),
            lax.rem(z + dz, Z),
            lax.rem(core + dc, 2),
        )

    xy_steps = sorted(((q % X, q // X) for q in range(n_xy)), key=lambda s: near(s[0], X) + near(s[1], Y))
    z_steps = sorted(range(Z), key=lambda q: -near(q, Z))
    zc_steps = [(dc, dz) for dc in (1, 0) for dz in z_steps]
    y_steps = sorted(range(Y), key=lambda q: -near(q, Y))
    blk_steps = sorted(
        ((dl, dz) for dl in range(YL) for dz in range(Z) if dl or dz), key=lambda s: -s[0] - near(s[1], Z)
    )
    edges = (0, min(5, n_xy - 2), min(11, n_xy - 1), n_xy)
    used = (0, min(5, n_xy - 2), min(10, n_xy - 1), n_xy)
    groups = [range(lo, hi) for lo, hi in zip(edges, edges[1:])]
    batches = [range(lo, hi) for lo, hi in zip(used, used[1:])]

    def yl_place(dl, dz):
        y_ = yh * YL + lax.rem(yl + dl, YL)
        return (x, y_, lax.rem(z + dz, Z), core)

    def send(send_s, recv_s, src, dst, place):
        pltpu.make_async_remote_copy(
            src_ref=src,
            dst_ref=dst,
            send_sem=send_sem.at[send_s],
            recv_sem=recv_sem.at[recv_s],
            device_id=device(*place),
            device_id_type=MESH,
        ).start()

    def wait_bytes(sem, ref):
        pltpu.make_async_copy(ref, ref, sem).wait()

    unfinished = []

    def finish():
        for phase, ref in unfinished:
            wait_bytes(send_sem.at[phase], ref)

    barrier = pltpu.get_barrier_semaphore()
    places = [shifted(dx=dx, dy=dy) for dx, dy in reversed(xy_steps[1:])]
    places += [shifted(dz=dz, dc=dc) for dc, dz in zc_steps[:-1]]
    places += [yl_place(dl, dz) for dl, dz in blk_steps if dl and dz]
    for place in places:
        pl.semaphore_signal(barrier, inc=1, device_id=device(*place), device_id_type=MESH)

    inputs = [
        pltpu.make_async_copy(src, dst, recv_sem.at[INP + i])
        for i, (src, dst) in enumerate(
            (
                (crd_hbm, crd_ref),
                (area_hbm, area_ref),
                (loads_hbm, loads_ref),
                (rec_hbm, rec_ref),
                (shp_hbm, shp_ref),
                (cpl_hbm, cpl_ref),
            )
        )
    ]
    for copy in inputs:
        copy.start()
    inputs[0].wait()
    inputs[1].wait()
    half_scale = 0.5 * WAVE / math.pi
    geo_s[0, 0:3, :] = crd_ref[...] * half_scale
    geo_s[0, 3:4, :] = area_ref[...] * (half_scale * half_scale / total_panels)
    geo_t[n_zc - 1, :, :] = geo_s[0, :, :]
    inputs[2].wait()
    inputs[3].wait()
    loads = loads_ref[...]
    loads_rot = rotated(loads.astype(F32)).astype(BF16)
    psum = jnp.dot(rec_ref[0], loads, preferred_element_type=F32) + jnp.dot(
        rec_ref[1], loads_rot, preferred_element_type=F32
    )
    part[...] = psum.reshape(n_blk, RW, CW)
    part_h[...] = psum.astype(BF16).reshape(n_blk, RW, CW)

    pl.semaphore_wait(barrier, len(places))

    for q, (dl, dz) in enumerate(blk_steps):
        place = yl_place(dl, dz)
        owner = lax.rem(place[1], YL) * Z + place[2]
        send(RS_AMP, RS_AMP, part_h.at[owner], amp_in.at[q], place)
    for n in range(1, n_xy):
        dx, dy = xy_steps[n]
        send(GEO_S, GEO_S, geo_s.at[0], geo_s.at[n], shifted(dx=dx, dy=dy))
    for t in range(n_zc - 1):
        dc, dz = zc_steps[t]
        send(GEO_T, GEO_T, geo_t.at[n_zc - 1], geo_t.at[t], shifted(dz=dz, dc=dc))
    unfinished.append((GEO_S, geo_s.at[pl.ds(1, n_xy - 1)]))
    unfinished.append((GEO_T, geo_t.at[pl.ds(1, n_zc - 1)]))
    unfinished.append((RS_AMP, amp_in))

    def prepare():
        inputs[4].wait()
        area_b[...] = turn_rows(area_ref[...])
        shp_f[...] = shp_ref[...].astype(F32).reshape(PB * KB, mb)
        for k in range(KB):
            block = shp_f[pl.ds(k, PB, stride=KB), :]
            shp_k[k] = block.astype(BF16)
            shp_t[k] = jnp.transpose(block).astype(BF16)
        cbuf[KB] = jnp.zeros((2, X, RW, CW), BF16)
        inputs[5].wait()

        def fill_inv(j, carry):
            found = jnp.int32(KB)
            for k in range(KB):
                found = jnp.where(cpl_ref[0, k] == j, jnp.int32(k), found)
            inv[j] = found
            return carry

        lax.fori_loop(0, n_blk * YH, fill_inv, 0)

    def turn_step(slot, carry):
        rows = pl.ds(pl.multiple_of(slot * PB, PB), PB)
        for axis in range(3):
            tgt_b[axis, rows, :] = turn_rows(geo_t[slot, axis : axis + 1, :])
        return carry

    steps = n_zc * PB // ROWS

    def kernel_chunks(lo, hi):
        def chunk(d, carry):
            shape = (ROWS, PB)
            sx = jnp.broadcast_to(geo_s[d, 0:1, :], shape)
            sy = jnp.broadcast_to(geo_s[d, 1:2, :], shape)
            sz = jnp.broadcast_to(geo_s[d, 2:3, :], shape)
            sa = jnp.broadcast_to(geo_s[d, 3:4, :], shape)

            def rows_step(i, inner):
                rows = pl.ds(pl.multiple_of(i * ROWS, ROWS), ROWS)
                dx = tgt_b[0, rows, :] - sx
                dy = tgt_b[1, rows, :] - sy
                dz = tgt_b[2, rows, :] - sz
                d2 = dx * dx + dy * dy + dz * dz + sa
                r = lax.rsqrt(d2)
                h = d2 * r
                f = h - jnp.round(h)
                u = f * f
                s = horner(SIN, u) * f
                c = horner(COS, u)
                rs = r * s
                kmat[d, rows, 0:PB] = (r - rs * s).astype(BF16)
                kmat[d, rows, PB : 2 * PB] = (rs * c).astype(BF16)
                return inner

            return lax.fori_loop(0, steps, rows_step, carry)

        lax.fori_loop(lo, hi, chunk, 0)

    cuts = [round(n_xy * part_of / 16) for part_of in CUTS]

    prepare()

    wait_bytes(recv_sem.at[RS_AMP], amp_in)
    asum = part[blk]
    for q in range(n_blk - 1):
        asum = asum + amp_in[q].astype(F32)
    xl = x * YL + yl
    amp[core, yh, xl, z] = asum.astype(BF16)
    for dz in z_steps[:-1]:
        mine = amp.at[core, yh, xl, z]
        send(AG_Z, AG_Z, mine, mine, shifted(dz=dz))
    seven = amp.at[0, 0, 0, pl.ds(0, Z - 1)]
    unfinished.append((AG_Z, seven))

    wait_bytes(recv_sem.at[GEO_T], geo_t.at[pl.ds(1, n_zc - 1)])
    lax.fori_loop(0, n_zc, turn_step, 0)
    wait_bytes(recv_sem.at[GEO_S], geo_s.at[pl.ds(1, n_xy - 1)])
    kernel_chunks(0, cuts[0])
    wait_bytes(recv_sem.at[AG_Z], seven)
    mine = amp.at[core, yh, xl]

    def send_block(g):
        for n in groups[g]:
            dx, dy = xy_steps[n]
            if n:
                send(AG_XY, AG_XY + g, mine, mine, shifted(dx=dx, dy=dy))

    send_block(2)
    send_block(1)
    kernel_chunks(cuts[0], cuts[1])
    send_block(0)
    unfinished.append((AG_XY, vels.at[pl.ds(1, n_xy - 1), pl.ds(0, mb)]))
    kernel_chunks(cuts[1], cuts[4])
    for g in (2, 1, 0):
        rest = [n for n in groups[g] if n]
        if rest:
            wait_bytes(recv_sem.at[AG_XY + g], vels.at[pl.ds(1, len(rest)), pl.ds(0, mb)])
    half_amp = amp.at[core]
    send(AG_C, AG_C, half_amp, half_amp, shifted(dc=1))
    unfinished.append((AG_C, half_amp))
    kernel_chunks(cuts[4], cuts[5])
    wait_bytes(recv_sem.at[AG_C], half_amp)

    vel = jnp.zeros((PB, CW), F32)
    for k in range(KB):
        j = cpl_ref[0, k]
        jl = lax.rem(j, X * YL)
        jc = lax.rem(lax.div(j, X * YL), 2)
        jh = lax.div(j, X * YL * 2)
        block = amp[jc, jh, jl].reshape(mb, CW)
        vel = vel + jnp.dot(shp_k[k], block, preferred_element_type=F32)
    vels[0] = (vel * area_b[...] * (half_scale / math.sqrt(total_panels))).astype(BF16)
    for g, group in enumerate(groups):
        for n in group:
            dx, dy = xy_steps[n]
            if n:
                batch = [n in b for b in batches].index(True)
                send(VEL, VEL + batch, vels.at[0], vels.at[n], shifted(dx=dx, dy=dy))
    kernel_chunks(cuts[5], n_xy)
    unfinished.append((VEL, vels.at[pl.ds(1, n_xy - 1)]))

    def weights(g):
        group = batches[g]
        rest = [n for n in group if n]
        if rest:
            wait_bytes(recv_sem.at[VEL + g], vels.at[pl.ds(rest[0], len(rest))])
        for n in group:
            value = vels[n]
            w_ref[n, 0:PB, :] = value
            w_ref[n, PB : 2 * PB, :] = rotated(value.astype(F32)).astype(BF16)

    def products(g, rows):
        total = None
        for n in batches[g]:
            term = jnp.dot(kmat[n, rows, :], w_ref[n], preferred_element_type=F32)
            total = term if total is None else total + term
        return total

    mm_rows = min(1024, n_zc * PB)
    last = len(batches) - 1
    for g in range(last):
        weights(g)

        def mm_step(i, carry):
            rows = pl.ds(pl.multiple_of(i * mm_rows, mm_rows), mm_rows)
            prod = products(g, rows)
            acc[rows, :] = prod if g == 0 else acc[rows, :] + prod
            return carry

        lax.fori_loop(0, n_zc * PB // mm_rows, mm_step, 0)

    weights(last)
    pair = 2
    n_pair = Z // pair

    def other_core(i):
        rows = pl.ds(pl.multiple_of(i * (pair * PB), pair * PB), pair * PB)
        value = acc[rows, :] + products(last, rows)
        p_out[i] = value.astype(BF16).reshape(pair, PB, CW)
        send(RS_PC, RS_PC + i, p_out.at[i], pc_in.at[i], shifted(dc=1))

    def this_core(i, final=False):
        rows = pl.ds(pl.multiple_of((n_pair + i) * (pair * PB), pair * PB), pair * PB)
        value = acc[rows, :] + products(last, rows)
        wait_bytes(recv_sem.at[RS_PC + i], pc_in.at[i])
        value = value + pc_in[i].astype(F32).reshape(pair * PB, CW)
        for h in range(pair):
            t = i * pair + h
            part_p = value[h * PB : (h + 1) * PB]
            if final and h == pair - 1:
                return part_p
            back = Z // 2 + i + 1 if h else Z // 2 - i
            pz_out[t] = part_p.astype(BF16)
            send(RS_PZ, RS_PZ, pz_out.at[t], pz_in.at[t], shifted(dz=back))

    def first_steps(i, carry):
        other_core(i)
        return carry

    def middle_steps(i, carry):
        other_core(i + ahead)
        this_core(i)
        return carry

    def later_steps(i, carry):
        this_core(i)
        return carry

    ahead = min(2, n_pair)
    lax.fori_loop(0, ahead, first_steps, 0)
    lax.fori_loop(0, n_pair - ahead, middle_steps, 0)
    lax.fori_loop(n_pair - ahead, n_pair - 1, later_steps, 0)
    total = this_core(n_pair - 1, final=True)
    unfinished.append((RS_PC, p_out))
    unfinished.append((RS_PZ, pz_in))
    wait_bytes(recv_sem.at[RS_PZ], pz_in)
    for t in range(Z - 1):
        total = total + pz_in[t].astype(F32)
    pressure = total.astype(BF16)
    prs_ref[...] = pressure
    weighted = (area_b[...] * pressure.astype(F32)).astype(BF16)

    for k in range(KB):
        cbuf[k] = (
            jnp.dot(shp_t[k], weighted, preferred_element_type=F32)
            .astype(BF16)
            .reshape(2, X, RW, CW)
        )
    other = 1 - core
    for n, dy in enumerate(y_steps):
        y_ = lax.rem(y + dy, Y)
        first = lax.rem(y_, YL) * (Z * YH) + lax.div(y_, YL)
        for zz in range(Z):
            lc_out[n, zz] = cbuf[inv[first + zz * YH], other]
        send(RS_LC, RS_LC + n, lc_out.at[n], lc_in.at[n], shifted(dc=1))
    unfinished.append((RS_LC, lc_out))
    lx_slot = 0
    for n, dy in enumerate(y_steps):
        y_ = lax.rem(y + dy, Y)
        first = lax.rem(y_, YL) * (Z * YH) + lax.div(y_, YL)
        wait_bytes(recv_sem.at[RS_LC + n], lc_in.at[n])
        for zz in range(Z):
            both = cbuf[inv[first + zz * YH], core].astype(F32) + lc_in[n, zz].astype(F32)
            for xx in range(X):
                lx_out[n, xx, zz] = both[xx].astype(BF16)
                if dy == 0:
                    lx_own[xx, zz] = both[xx]
        for dx in sorted(range(X), key=lambda q: -near(q, X)):
            if dx or dy:
                place = shifted(dx=dx, dy=dy)
                send(RS_LXY, RS_LXY, lx_out.at[n, place[0]], lx_in.at[lx_slot], place)
                lx_slot += 1
    unfinished.append((RS_LXY, lx_in))
    wait_bytes(recv_sem.at[RS_LXY], lx_in)
    lsum = lx_own[x]
    for q in range(n_xy - 1):
        lsum = lsum + lx_in[q].astype(F32)
    lx_own[x] = lsum
    lz_out[...] = lsum.astype(BF16)
    for t, dz in enumerate(z_steps[:-1]):
        place = shifted(dz=dz)
        send(RS_LZ, RS_LZ, lz_out.at[place[2]], lz_in.at[t], place)
    unfinished.append((RS_LZ, lz_in))
    fin = lx_own[x, z]
    wait_bytes(recv_sem.at[RS_LZ], lz_in)
    for t in range(Z - 1):
        fin = fin + lz_in[t].astype(F32)
    out_ref[...] = fin
    finish()


def copy_kernel(a_ref, b_ref, c_ref, d_ref):
    c_ref[...] = a_ref[...]
    d_ref[...] = b_ref[...]


def solution(mesh):
    Z = mesh.shape["blk"] // YL
    YH = mesh.shape["tgt"] // 2
    X = mesh.shape["sec"]
    Y = YH * YL
    n_xy, n_zc, n_blk = X * Y, 2 * Z, YL * Z
    mb = Z * RW

    def on_device(modal_loads, receptance, shapes, coupling, panel_coords, panel_areas):
        KB = shapes.shape[1]
        scratch = [
            pltpu.VMEM(modal_loads.shape, BF16),
            pltpu.VMEM(receptance.shape, BF16),
            pltpu.VMEM(shapes.shape, BF16),
            pltpu.SMEM(coupling.shape, jnp.int32),
            pltpu.VMEM(panel_coords.shape, F32),
            pltpu.VMEM((1, PB), F32),
            pltpu.VMEM((n_xy, 4, PB), F32),
            pltpu.VMEM((n_zc, 4, PB), F32),
            pltpu.VMEM((3, n_zc * PB, PB), F32),
            pltpu.VMEM((PB, PB), F32),
            pltpu.VMEM((n_xy, n_zc * PB, 2 * PB), BF16),
            pltpu.VMEM((n_zc * PB, CW), F32),
            pltpu.VMEM((n_blk, RW, CW), F32),
            pltpu.VMEM((n_blk, RW, CW), BF16),
            pltpu.VMEM((n_blk - 1, RW, CW), BF16),
            pltpu.VMEM((2, YH, X * YL, Z, RW, CW), BF16),
            pltpu.VMEM((n_xy, PB, CW), BF16),
            pltpu.VMEM((n_xy, 2 * PB, CW), BF16),
            pltpu.VMEM((Z // 2, 2, PB, CW), BF16),
            pltpu.VMEM((Z // 2, 2, PB, CW), BF16),
            pltpu.VMEM((Z - 1, PB, CW), BF16),
            pltpu.VMEM((Z - 1, PB, CW), BF16),
            pltpu.VMEM((PB * KB, mb), F32),
            pltpu.VMEM((KB, PB, mb), BF16),
            pltpu.VMEM((KB, mb, PB), BF16),
            pltpu.SMEM((n_blk * YH,), jnp.int32),
            pltpu.VMEM((KB + 1, 2, X, RW, CW), BF16),
            pltpu.VMEM((Y, Z, X, RW, CW), BF16),
            pltpu.VMEM((Y, Z, X, RW, CW), BF16),
            pltpu.VMEM((Y, X, Z, RW, CW), BF16),
            pltpu.VMEM((n_xy - 1, Z, RW, CW), BF16),
            pltpu.VMEM((X, Z, RW, CW), F32),
            pltpu.VMEM((Z, RW, CW), BF16),
            pltpu.VMEM((Z - 1, RW, CW), BF16),
            pltpu.SemaphoreType.DMA((N_SEM,)),
            pltpu.SemaphoreType.DMA((N_SEM,)),
        ]
        vmem = pl.BlockSpec(memory_space=pltpu.VMEM)
        outs = (
            jax.ShapeDtypeStruct((RW, CW), F32),
            jax.ShapeDtypeStruct((PB, CW), BF16),
        )
        results = pl.pallas_call(
            functools.partial(kernel, (X, YH, Z, KB)),
            out_shape=outs,
            in_specs=[pl.BlockSpec(memory_space=pl.ANY)] * 6,
            out_specs=(vmem, vmem),
            scratch_shapes=scratch,
            compiler_params=pltpu.CompilerParams(
                collective_id=0,
                has_side_effects=True,
                vmem_limit_bytes=58 * 1024 * 1024,
            ),
        )(
            modal_loads,
            receptance,
            shapes,
            coupling,
            panel_coords,
            panel_areas.reshape(1, PB),
        )
        return pl.pallas_call(
            copy_kernel,
            out_shape=outs,
            in_specs=[vmem, vmem],
            out_specs=(vmem, vmem),
        )(*results)

    owned = ("blk", "tgt", "sec")
    in_specs = (
        P("blk", None),
        P(None, ("tgt", "sec"), "blk"),
        P(owned, None, None),
        P(owned, None),
        P(None, owned),
        P(owned),
    )
    return jax.shard_map(
        on_device,
        mesh=mesh,
        in_specs=in_specs,
        out_specs=(P(owned, None), P(owned, None)),
        check_vma=False,
    )
```
